256 devices in a mesh: src: 8 (over z_hi, y), tile: 32 (over z_lo, x, core).
Axes of the slice: x: 4, y: 4, z: 8 (z_hi: 2, z_lo: 4; z = z_hi * 4 + z_lo), core: 2. Of those that a mesh axis runs over, the one named last changes fastest.
Arguments:
- mask_tiles: bfloat16 [32, 1024, 1024], P('tile'), may hold values from -6 to 6
- slot_pos: int32 [32], replicated, may hold values from 0 to 31, as said below
- src_shift: int32 [16, 2], P('src'), may hold values from -32 to 32
- src_weight: int32 [16], P('src'), may hold values from 1 to 8
- pupil_phase: float32 [128, 128], replicated, may hold values from -3.140625 to 3.140625
- target: bfloat16 [32, 1024, 1024], P('tile'), may hold values from 0 to 1
Outputs:
- resist: float32 [32, 1024, 1024], P('tile', 'src')
- mask_step: float32 [32, 1024, 1024], P('tile', 'src')
The draws below stay inside these ranges and needn't reach their ends.
Inputs may be any that keep to these rules, and one draw needn't show every extreme that they name: slot_pos is a permutation of the strip positions.
All inputs are finite; a program needn't handle non-finite values.
Results may differ from the reference program's by a relative error of at most 0.0051.
Values may be sent and summed in bfloat16 or wider, within the bound.
No kernel may reach another device: no remote copies, remote signals or barrier semaphores. Data moves between devices by JAX's collectives and lax.ppermute only.
A program may use at most 128 MiB of HBM per device.

```python
import math
import jax
import jax.numpy as jnp
from jax import lax

TILE_PX = 1024
HALO = 64
FREQ = 128
PUPIL_R = 28
SHIFT_MAX = 32
SOURCES = 16
TILES = 32
EXT_PX = 1152


def draw_slot_pos(key, part):
    order_key = jax.random.fold_in(key, 11)
    pick_key = jax.random.fold_in(key, 23)
    order = jax.random.permutation(order_key, TILES).astype(jnp.int32)
    half_count = TILES // 2
    first_slot = jax.random.randint(pick_key, (), 0, half_count).astype(jnp.int32)
    second_slot = first_slot + half_count
    first_value = order[first_slot]
    wanted = jnp.where(first_value == TILES - 1, first_value - 1, first_value + 1).astype(jnp.int32)
    where_wanted = jnp.argmax((order == wanted).astype(jnp.int32)).astype(jnp.int32)
    second_value = order[second_slot]
    order = order.at[where_wanted].set(second_value)
    order = order.at[second_slot].set(wanted)
    return order


def touch_ends(drawn, own_key, smallest, high):
    place = [jax.random.randint(jax.random.fold_in(own_key, axis), (), 0, length) for axis, length in enumerate(drawn.shape)]
    widest = drawn.shape.index(max(drawn.shape))
    neighbour = place[:widest] + [(place[widest] + 1) % drawn.shape[widest]] + place[widest + 1:]
    return drawn.at[tuple(place)].set(smallest).at[tuple(neighbour)].set(high)


def block_levels(own_key, extent, split, smallest, largest):
    level, own = 1.0, jax.random.fold_in(own_key, 6)
    for position, shards_of in split:
        heights = jnp.exp(jax.random.uniform(jax.random.fold_in(own, position), (shards_of,), jnp.float32, smallest / len(split), largest / len(split)))
        level = level * jnp.repeat(heights, extent[position] // shards_of).reshape([-1 if axis == position else 1 for axis in range(len(extent))])
    return level


def noise(key, extent, deviation, reach, cuts=(), kind=jnp.bfloat16):
    entries = deviation * jax.random.normal(key, extent, jnp.float32)
    if cuts:
        entries = entries * block_levels(key, extent, cuts, -0.22, 0.18)
    return jnp.clip(entries, -reach, reach).astype(kind)


def setup_inputs(seed: int = 0) -> dict:
    splits = jax.random.split(jax.random.key(seed), 7)
    mask_tiles = noise(splits[0], (TILES, TILE_PX, TILE_PX), 1.0, 6.0, ((0, 32),))
    slot_pos = draw_slot_pos(jax.random.fold_in(splits[6], 71), 0)
    src_shift = touch_ends(jax.random.randint(splits[2], (SOURCES, 2), 0 - SHIFT_MAX, SHIFT_MAX + 1), jax.random.fold_in(splits[2], 1), 0 - SHIFT_MAX, SHIFT_MAX).astype(jnp.int32)
    src_weight = touch_ends(jax.random.randint(splits[3], (SOURCES,), 1, 9), jax.random.fold_in(splits[3], 1), 1, 8).astype(jnp.int32)
    pupil_phase = jnp.clip(jax.random.uniform(splits[4], (FREQ, FREQ), jnp.float32, -3.140625, 3.140625), -3.140625, 3.140625)
    target = jnp.clip(1.0 * jax.random.uniform(splits[5], (TILES, TILE_PX, TILE_PX), jnp.float32) ** block_levels(splits[5], (TILES, TILE_PX, TILE_PX), ((0, 32),), -0.2, 0.2), 0.0, 1.0).astype(jnp.bfloat16)
    return dict(mask_tiles=mask_tiles, slot_pos=slot_pos, src_shift=src_shift, src_weight=src_weight, pupil_phase=pupil_phase, target=target)


steepness = 4.0
threshold = 0.6
learn_rate = 8.0

def hdot(left, right):
    return jnp.dot(left, right, precision=lax.Precision.HIGHEST, preferred_element_type=jnp.float32)

def angle_table(positions, frequency, period):
    wrapped = jnp.mod(positions[:, None] * frequency[None, :], period)
    return wrapped.astype(jnp.float32) * (2.0 * math.pi / period)

def pupil_parts(shift_pair, pupil_phase, frequency):
    padded = jnp.pad(pupil_phase, FREQ)
    shift_a = shift_pair[0].astype(jnp.int32)
    shift_b = shift_pair[1].astype(jnp.int32)
    window = lax.dynamic_slice(padded, (FREQ + shift_a, FREQ + shift_b), (FREQ, FREQ))
    along_bins = frequency + shift_a
    across = frequency + shift_b
    inside = along_bins[:, None] * along_bins[:, None] + across[None, :] * across[None, :] <= PUPIL_R * PUPIL_R
    return (jnp.where(inside, jnp.cos(window), 0.0), jnp.where(inside, jnp.sin(window), 0.0))

def reference(mask_tiles, slot_pos, src_shift, src_weight, pupil_phase, target):
    frequency = jnp.arange(FREQ, dtype=jnp.int32) - FREQ // 2
    col_angles = angle_table(jnp.arange(TILE_PX, dtype=jnp.int32), frequency, TILE_PX)
    col_cos = jnp.cos(col_angles)
    col_sin = jnp.sin(col_angles)
    col_cos_b = col_cos.astype(jnp.bfloat16)
    col_sin_b = col_sin.astype(jnp.bfloat16)
    col_both = jnp.concatenate([col_cos_b, col_sin_b], axis=1)
    col_cos_bt = col_cos_b.astype(jnp.float32).T
    col_sin_bt = col_sin_b.astype(jnp.float32).T
    row_angles = angle_table(jnp.arange(EXT_PX, dtype=jnp.int32), frequency, EXT_PX)
    row_cos = jnp.cos(row_angles)
    row_sin = jnp.sin(row_angles)
    out_angles = angle_table(jnp.arange(TILE_PX, dtype=jnp.int32) + HALO, frequency, EXT_PX)
    out_table = jnp.concatenate([jnp.cos(out_angles), jnp.sin(out_angles)], axis=1).astype(jnp.bfloat16)
    scale_factor = 1.0 / (FREQ / 2 * math.sqrt(EXT_PX * TILE_PX))
    holder = jnp.zeros((TILES,), jnp.int32).at[slot_pos].set(jnp.arange(TILES, dtype=jnp.int32))
    clip_mask = mask_tiles[holder]
    clip_target = target[holder]
    rim_zeros = jnp.zeros((1, HALO, TILE_PX), jnp.bfloat16)
    upper_rim = jnp.concatenate([rim_zeros, clip_mask[:-1, TILE_PX - HALO:]], axis=0)
    lower_rim = jnp.concatenate([clip_mask[1:, :HALO], rim_zeros], axis=0)
    patches = jnp.concatenate([upper_rim, clip_mask, lower_rim], axis=1)
    pupils_re, pupils_im = jax.vmap(lambda pair: pupil_parts(pair, pupil_phase, frequency))(src_shift)
    weights = src_weight.astype(jnp.float32) / (4.0 * SOURCES)

    def tile_work(inputs):
        tile_patch, tile_target = inputs
        half_spec = jnp.dot(tile_patch, col_both, preferred_element_type=jnp.float32)
        half_re = half_spec[:, :FREQ]
        half_im = -half_spec[:, FREQ:]
        spec_re = hdot(row_cos.T, half_re) + hdot(row_sin.T, half_im)
        spec_im = hdot(row_cos.T, half_im) - hdot(row_sin.T, half_re)

        def make_stack(pupil_re, pupil_im):
            amp_re = scale_factor * (pupil_re * spec_re - pupil_im * spec_im)
            amp_im = scale_factor * (pupil_re * spec_im + pupil_im * spec_re)
            line_re = (hdot(amp_re, col_cos.T) - hdot(amp_im, col_sin.T)).astype(jnp.bfloat16)
            line_im = (hdot(amp_re, col_sin.T) + hdot(amp_im, col_cos.T)).astype(jnp.bfloat16)
            top_half = jnp.concatenate([line_re, line_im], axis=1)
            low_half = jnp.concatenate([-line_im, line_re], axis=1)
            return jnp.concatenate([top_half, low_half], axis=0)
        stacks = jax.vmap(make_stack)(pupils_re, pupils_im)

        def add_image(total_image, inputs):
            line_stack, weight = inputs
            field_rows = jnp.dot(out_table, line_stack, preferred_element_type=jnp.float32)
            squared = field_rows * field_rows
            return (total_image + weight * (squared[:, :TILE_PX] + squared[:, TILE_PX:]), None)
        intensity = lax.scan(add_image, jnp.zeros((TILE_PX, TILE_PX), jnp.float32), (stacks, weights))[0]
        resist_tile = jax.nn.sigmoid(steepness * (intensity - threshold))
        adjoint = (2.0 * (resist_tile - tile_target.astype(jnp.float32)) * steepness * resist_tile * (1.0 - resist_tile)).astype(jnp.bfloat16)
        adjoint_wide = jnp.concatenate([adjoint, adjoint], axis=1).astype(jnp.float32)

        def add_grad(totals, inputs):
            line_stack, weight, pupil_re, pupil_im = inputs
            field_rows = jnp.dot(out_table, line_stack, preferred_element_type=jnp.float32)
            dfield = (2.0 * weight * adjoint_wide * field_rows).astype(jnp.bfloat16)
            blocks = lax.dot_general(out_table, dfield, (((0,), (0,)), ((), ())), preferred_element_type=jnp.float32)
            dline_re = blocks[:FREQ, :TILE_PX] + blocks[FREQ:, TILE_PX:]
            dline_im = blocks[:FREQ, TILE_PX:] - blocks[FREQ:, :TILE_PX]
            damp_re = hdot(dline_re, col_cos) + hdot(dline_im, col_sin)
            damp_im = hdot(dline_im, col_cos) - hdot(dline_re, col_sin)
            grad_re = totals[0] + scale_factor * (pupil_re * damp_re + pupil_im * damp_im)
            grad_im = totals[1] + scale_factor * (pupil_re * damp_im - pupil_im * damp_re)
            return ((grad_re, grad_im), None)
        empty = jnp.zeros((FREQ, FREQ), jnp.float32)
        grads = lax.scan(add_grad, (empty, empty), (stacks, weights, pupils_re, pupils_im))[0]
        return (resist_tile, grads[0], grads[1])
    resist_clip, grads_re, grads_im = lax.map(tile_work, (patches, clip_target))

    def patch_gradient(inputs):
        grad_re, grad_im = inputs
        back_re = hdot(row_cos, grad_re) - hdot(row_sin, grad_im)
        back_im = hdot(row_sin, grad_re) + hdot(row_cos, grad_im)
        return hdot(back_re, col_cos_bt) - hdot(back_im, col_sin_bt)
    patch_grads = lax.map(patch_gradient, (grads_re, grads_im))
    zero_rows = jnp.zeros((1, HALO, TILE_PX), jnp.float32)
    inner_rows = patch_grads[:, HALO:HALO + TILE_PX]
    from_above = jnp.concatenate([zero_rows, patch_grads[:-1, TILE_PX + HALO:]], axis=0)
    from_below = jnp.concatenate([patch_grads[1:, :HALO], zero_rows], axis=0)
    step_clip = inner_rows.at[:, :HALO].add(from_above).at[:, TILE_PX - HALO:].add(from_below)
    return (resist_clip[slot_pos], -learn_rate * step_clip[slot_pos])
```

```python
import math
import numpy as np, jax, jax.numpy as jnp
from jax import lax
from jax.sharding import PartitionSpec as P

HI=lax.Precision.HIGHEST
def hdot(a,b): return jnp.dot(a,b,precision=HI,preferred_element_type=jnp.float32)
k=np.arange(64)
def tab(pos,period):
    ang=2*np.pi*((pos[:,None]*k[None])%period)/period
    return np.concatenate([np.cos(ang),np.sin(ang)],1)
TC=tab(np.arange(1024),1024); TR=tab(np.arange(1152),1152)
f=np.arange(128)-64
Ec=np.zeros((128,64)); Es=np.zeros((128,64))
for i,ff in enumerate(f):
    if ff==-64: continue
    Ec[i,abs(ff)]=1; Es[i,abs(ff)]=np.sign(ff)
E=np.concatenate([Ec,Es],1)
ap=np.arange(64)-32
ang=2*np.pi*((np.arange(128)[:,None]*ap[None])%128)/128
Wr,Wi=np.cos(ang),np.sin(ang)
WX=np.concatenate([np.concatenate([Wr.T,Wi.T],1),np.concatenate([-Wi.T,Wr.T],1)],0)
WY=np.concatenate([np.concatenate([Wr,-Wi],1),np.concatenate([Wi,Wr],1)],0)
def interp(pos):
    p=np.arange(-63,64)
    d=pos[:,None]-np.arange(128)[None]
    return np.cos(2*np.pi*d[:,:,None]*p/128).sum(-1)/128
RY=interp((64+np.arange(1024))/9.0); RX=interp(np.arange(1024)/8.0)
disc=(ap[:,None]**2+ap[None]**2<=784)
scale=1.0/(64*math.sqrt(1152*1024))
sg=np.ones((128,128));
Mre=np.zeros((128,128)); Mre[:64,:64]=1; Mre[64:,64:]=-1
Mim=np.zeros((128,128)); Mim[:64,64:]=-1; Mim[64:,:64]=-1
c32=lambda a: jnp.asarray(a,jnp.float32)
def main(M,shifts,weights,phase,target):
    e=c32(E)
    sre=hdot(hdot(e,M*c32(Mre)),e.T); sim=hdot(hdot(e,M*c32(Mim)),e.T)
    ph=phase[32:96,32:96]
    pr=jnp.where(disc,jnp.cos(ph),0)*scale; pi=jnp.where(disc,jnp.sin(ph),0)*scale
    ki=jnp.arange(128)
    U=(ki[None,None,:]==(jnp.arange(64)[None,:,None]+32-shifts[:,0,None,None])).astype(jnp.float32)
    V=(ki[None,None,:]==(jnp.arange(64)[None,:,None]+32-shifts[:,1,None,None])).astype(jnp.float32)
    ein=lambda s,*a: jnp.einsum(s,*a,precision=HI,preferred_element_type=jnp.float32)
    wr=ein('sal,sbl->sab',ein('sak,kl->sal',U,sre),V); wi=ein('sal,sbl->sab',ein('sak,kl->sal',U,sim),V)
    A=jnp.concatenate([pr*wr-pi*wi,pr*wi+pi*wr],2)
    L=ein('sak,kj->saj',A,c32(WX))
    L2=jnp.concatenate([L[:,:,:128],L[:,:,128:]],1)
    g=ein('ik,skj->sij',c32(WY),L2)
    sq=g*g
    Ic=(weights[:,None,None]*(sq[:,:128]+sq[:,128:])).sum(0)
    I=hdot(hdot(c32(RY),Ic),c32(RX).T)
    r=jax.nn.sigmoid(4.0*(I-0.6))
    adj=(2.0*(r-target.astype(jnp.float32))*4.0*r*(1-r)).astype(jnp.bfloat16).astype(jnp.float32)
    Ac=hdot(hdot(c32(RY).T,adj),c32(RX))
    dg=g*(2*weights[:,None,None]*jnp.concatenate([Ac,Ac],0))
    dL2=ein('ik,sij->skj',c32(WY),dg)
    dL=jnp.concatenate([dL2[:,:64],dL2[:,64:]],2)
    dA=ein('saj,kj->sak',dL,c32(WX))
    dr,di=dA[:,:,:64],dA[:,:,64:]
    gr=pr*dr+pi*di; gi=pr*di-pi*dr
    Gr=ein('sak,sal->kl',U,ein('sab,sbl->sal',gr,V)); Gi=ein('sak,sal->kl',U,ein('sab,sbl->sal',gi,V))
    N=hdot(hdot(e.T,Gr),e)*c32(Mre)+hdot(hdot(e.T,Gi),e)*c32(Mim)
    return r,N


def per_device(mask_tiles, slot_pos, src_shift, src_weight, pupil_phase, target):
    tile_count = lax.axis_size("tile")
    src_count = lax.axis_size("src")
    my_slot = lax.axis_index("tile")
    my_src = lax.axis_index("src")
    row_share = 1024 // src_count
    slot_ids = jnp.arange(tile_count, dtype=jnp.int32)
    my_position = jnp.sum(jnp.where(slot_ids == my_slot, slot_pos, 0))
    is_above = slot_pos == my_position - 1
    is_below = slot_pos == my_position + 1
    ints = jnp.concatenate([src_shift, src_weight[:, None]], axis=1)
    step = 1
    while step < src_count:
        other = lax.ppermute(ints, "src", [(i, i ^ step) for i in range(src_count)])
        ints = jnp.concatenate([ints, other], axis=0)
        step *= 2
    weights = ints[:, 2].astype(jnp.float32) / (4.0 * ints.shape[0])
    col_table = jnp.asarray(TC, jnp.float32).astype(jnp.bfloat16)
    row_table = c32(TR)
    half = jnp.dot(mask_tiles[0], col_table, preferred_element_type=jnp.float32)
    rims = half.astype(jnp.bfloat16)
    sent = jnp.where(is_below[:, None, None], rims[None, 960:],
                     jnp.where(is_above[:, None, None], rims[None, :64], jnp.bfloat16(0)))
    got = lax.all_to_all(sent, "tile", 0, 0, tiled=True).astype(jnp.float32)
    upper = jnp.sum(jnp.where(is_above[:, None, None], got, 0.0), axis=0)
    lower = jnp.sum(jnp.where(is_below[:, None, None], got, 0.0), axis=0)
    moments = hdot(row_table.T, jnp.concatenate([upper, half, lower], axis=0))
    resist, folded = main(moments, ints[:, :2], weights, pupil_phase, target[0])
    edge_rows = jnp.where(my_src == 0, row_table[1088:], row_table[:64])
    edge_to = jnp.where(my_src == 0, is_below, is_above)
    edge = hdot(edge_rows, folded).astype(jnp.bfloat16)
    sent = jnp.where(edge_to[:, None, None], edge[None], jnp.bfloat16(0))
    got = lax.all_to_all(sent, "tile", 0, 0, tiled=True).astype(jnp.float32)
    edge_from = jnp.where(my_src == 0, is_above, is_below)
    wanted = (my_src == 0) | (my_src == src_count - 1)
    rim = jnp.sum(jnp.where((edge_from & wanted)[:, None, None], got, 0.0), axis=0)
    empty = jnp.zeros((row_share - 64, 128), jnp.float32)
    rim = jnp.where(my_src == 0, jnp.concatenate([rim, empty], axis=0), jnp.concatenate([empty, rim], axis=0))
    mine = lax.dynamic_slice_in_dim(row_table, 64 + my_src * row_share, row_share, 0)
    back = hdot(mine, folded) + rim
    step_rows = hdot(back, col_table.astype(jnp.float32).T)
    resist_rows = lax.dynamic_slice_in_dim(resist, my_src * row_share, row_share, 0)
    return (resist_rows[None], (-8.0 * step_rows)[None])


def solution(mesh):
    return jax.shard_map(
        per_device,
        mesh=mesh,
        in_specs=(P("tile", None, None), P(), P("src", None), P("src"), P(), P("tile", None, None)),
        out_specs=(P("tile", "src", None), P("tile", "src", None)),
        check_vma=False,
    )
```

```python
import math

import jax
import jax.numpy as jnp
import ml_dtypes
import numpy as np
from jax import lax
from jax.experimental import pallas as pl
from jax.experimental.pallas import tpu as pltpu
from jax.sharding import PartitionSpec as P

TILE_PX = 1024
HALO = 64
EXT_PX = 1152
FREQ = 128
GRID = 128
SOURCES = 16
PUPIL_R = 28
ROWS = 128
STEEPNESS = 4.0
THRESHOLD = 0.6
LEARN_RATE = 8.0
SCALE = 1.0 / (FREQ / 2 * math.sqrt(EXT_PX * TILE_PX))
INTERPRET = False
BF16 = ml_dtypes.bfloat16


def split(table):
    high = table.astype(BF16)
    return high, (table - high.astype(np.float64)).astype(BF16)


def half_table(count, period):
    angle = 2 * np.pi * ((np.arange(count)[:, None] * np.arange(64)[None]) % period) / period
    return np.concatenate([np.cos(angle), np.sin(angle)], axis=1)


def full_table(count, period):
    freq = np.arange(FREQ) - FREQ // 2
    angle = 2 * np.pi * ((np.arange(count)[:, None] * freq[None]) % period) / period
    keep = (freq > -64)[None]
    return np.concatenate([np.cos(angle) * keep, np.sin(angle) * keep], axis=1)


def unfold_tables():
    even = np.zeros((FREQ, 64))
    odd = np.zeros((FREQ, 64))
    for row, freq in enumerate(range(-64, 64)):
        if freq > -64:
            even[row, abs(freq)] = 1
            odd[row, abs(freq)] = np.sign(freq)
    return even, odd


def coarse_table():
    angle = 2 * np.pi * ((np.arange(GRID)[:, None] * (np.arange(64) - 32)[None]) % GRID) / GRID
    return np.cos(angle), np.sin(angle)


def interpolation(positions):
    apart = positions[:, None] - np.arange(GRID)[None]
    return np.cos(2 * np.pi * apart[:, :, None] * np.arange(-63, 64) / GRID).sum(axis=-1) / GRID


COL = half_table(TILE_PX, TILE_PX).astype(BF16)
ROW = full_table(EXT_PX, EXT_PX)
EVEN, ODD = unfold_tables()
COS_W, SIN_W = coarse_table()
ROW_F32 = ROW.astype(np.float32)
RIM_HL = np.concatenate(split(np.concatenate([ROW[:HALO], ROW[EXT_PX - HALO :]], axis=0).T), axis=1)
UNFOLD = np.stack(
    [
        np.concatenate([np.concatenate([EVEN, -ODD], axis=1).T] * 2, axis=0),
        np.concatenate([np.concatenate([-EVEN, -ODD], axis=1).T] * 2, axis=0),
        np.concatenate([np.concatenate([EVEN, ODD], axis=1)] * 2, axis=0),
    ]
).astype(BF16)
LEFT_H, LEFT_L = split(np.concatenate([COS_W, SIN_W], axis=0))
LEFT = np.concatenate([LEFT_H, LEFT_H, LEFT_L], axis=1)
RIGHT_H, RIGHT_L = split(
    np.concatenate(
        [np.concatenate([COS_W.T, SIN_W.T], axis=1), np.concatenate([-SIN_W.T, COS_W.T], axis=1)], axis=0
    )
)
RIGHT = np.concatenate([RIGHT_H, RIGHT_L], axis=0)
RIGHT_T = np.concatenate([RIGHT_H.T, RIGHT_L.T], axis=1)
LEFT_T = np.concatenate(split(np.concatenate([COS_W.T, SIN_W.T], axis=0)), axis=0)
GRID_Y = np.concatenate(split(interpolation((HALO + np.arange(TILE_PX)) / 9.0)), axis=1)
GRID_YT = np.concatenate(split(interpolation((HALO + np.arange(TILE_PX)) / 9.0).T), axis=0)
GRID_X = np.concatenate(split(interpolation(np.arange(TILE_PX) / 8.0)), axis=1)
DISC = (np.arange(64)[:, None] - 32) ** 2 + (np.arange(64)[None] - 32) ** 2 <= PUPIL_R * PUPIL_R


def dot(left, right):
    return jnp.dot(left, right, preferred_element_type=jnp.float32)


def dot_t(left, right):
    return lax.dot_general(left, right, (((1,), (1,)), ((), ())), preferred_element_type=jnp.float32)


def halves(value):
    high = value.astype(jnp.bfloat16)
    return high, (value - high.astype(jnp.float32)).astype(jnp.bfloat16)


def low_lanes(shape):
    return lax.broadcasted_iota(jnp.int32, shape, 1) < 64


def rims_kernel(where_ref, tile_ref, col_ref, sent_ref, rows_ref, sems):
    copies = [
        pltpu.make_async_copy(tile_ref.at[pl.ds(start, HALO)], rows_ref.at[pl.ds(place, HALO)], sems.at[number])
        for number, (start, place) in enumerate(((0, 0), (TILE_PX - HALO, HALO)))
    ]
    for copy in copies:
        copy.start()
    sent_ref[...] = jnp.zeros(sent_ref.shape, jnp.bfloat16)
    for copy in copies:
        copy.wait()
    rims = dot(rows_ref[...], col_ref[...]).astype(jnp.bfloat16)

    @pl.when(where_ref[2] > 0)
    def _():
        sent_ref[where_ref[0]] = rims[:HALO]

    @pl.when(where_ref[3] > 0)
    def _():
        sent_ref[where_ref[1]] = rims[HALO:]


def make_rims(where, tile, col):
    return pl.pallas_call(
        rims_kernel,
        out_shape=jax.ShapeDtypeStruct((32, HALO, 128), jnp.bfloat16),
        in_specs=[
            pl.BlockSpec(memory_space=pltpu.SMEM),
            pl.BlockSpec(memory_space=pl.ANY),
            pl.BlockSpec(memory_space=pltpu.VMEM),
        ],
        out_specs=pl.BlockSpec(memory_space=pltpu.VMEM),
        scratch_shapes=[pltpu.VMEM((2 * HALO, TILE_PX), jnp.bfloat16), pltpu.SemaphoreType.DMA((2,))],
        interpret=INTERPRET,
        name="rims",
    )(where, tile, col)


def fields_kernel(
    where_ref, ints_ref, up_ref, down_ref, own_ref, pupil_ref, rim_ref, unfold_ref, left_ref, right_ref, right_t_ref,
    left_t_ref, grid_y_ref, grid_yt_ref, grid_x_ref, edge_ref, mine_a_ref, mine_b_ref, target_hbm,
    resist_hbm, back_ref, sent_ref,
    target_ref, resist_ref, spec_ref, field_ref, fold_ref, grad_ref, sems,
):
    fetch = pltpu.make_async_copy(target_hbm, target_ref, sems.at[0])
    fetch.start()
    low = low_lanes((128, 128))
    low_w = low_lanes((64, 128))
    up = jnp.where(where_ref[2] > 0, up_ref[0].astype(jnp.float32), 0.0)
    down = jnp.where(where_ref[3] > 0, down_ref[0].astype(jnp.float32), 0.0)
    rims = jnp.concatenate([up, down], axis=0).astype(jnp.bfloat16)
    half = own_ref[...] + dot(rim_ref[...], jnp.concatenate([rims, rims], axis=0))
    by_cos, by_sin = half[:FREQ], half[FREQ:]
    spec_ref[0] = dot(jnp.concatenate(halves(jnp.where(low, by_cos, by_sin)), axis=1), unfold_ref[0])
    spec_ref[1] = dot(jnp.concatenate(halves(jnp.where(low, by_sin, by_cos)), axis=1), unfold_ref[1])
    coarse = jnp.zeros((GRID, GRID), jnp.float32)
    for source in range(SOURCES):
        shift_a = ints_ref[source, 0]
        shift_b = ints_ref[source, 1]
        rows = pl.ds(32 - shift_a, 64)
        spec_re = spec_ref[0, rows, :]
        spec_im = spec_ref[1, rows, :]
        near = lax.rem(96 + shift_b, 128)
        far = 32 + shift_b
        window = jnp.where(low_w, pltpu.roll(spec_re, near, 1), pltpu.roll(spec_im, far, 1))
        amp = pupil_ref[0] * window + pupil_ref[1] * pltpu.roll(window, 64, 1)
        amp_h, amp_l = halves(amp)
        both = dot(left_ref[...], jnp.concatenate([amp_h, amp_l, amp_h], axis=0))
        swapped = pltpu.roll(both[GRID:], 64, 1)
        line = both[:GRID] + jnp.where(low, -swapped, swapped)
        line_h, line_l = halves(line)
        field = dot(jnp.concatenate([line_h, line_h], axis=1), right_ref[...]) + dot(line_l, right_ref[:128])
        field_ref[source] = field
        weight = ints_ref[source, 2].astype(jnp.float32) * (1.0 / (4.0 * SOURCES))
        squared = field * field
        coarse = coarse + weight * (squared[:, :GRID] + squared[:, GRID:])
    coarse_h, coarse_l = halves(coarse)
    coarse_hh = jnp.concatenate([coarse_h, coarse_h], axis=0)
    fetch.wait()
    chunk = 256
    for place in range(TILE_PX // chunk):
        rows = pl.ds(place * chunk, chunk)
        rows_y = dot(grid_y_ref[rows, :], coarse_hh) + dot(grid_y_ref[rows, :GRID], coarse_l)
        rows_h, rows_l = halves(rows_y)
        intensity = dot_t(jnp.concatenate([rows_h, rows_h], axis=1), grid_x_ref[...]) + dot_t(
            rows_l, grid_x_ref[:, :GRID]
        )
        resist = jax.nn.sigmoid(STEEPNESS * (intensity - THRESHOLD))
        resist_ref[rows, :] = resist
        wanted = target_ref[rows, :].astype(jnp.float32)
        adjoint = ((2.0 * STEEPNESS) * (resist - wanted) * resist * (1.0 - resist)).astype(jnp.bfloat16)
        folded = dot(adjoint, grid_x_ref[...])
        fold_ref[rows, :] = jnp.concatenate(halves(folded[:, :GRID] + folded[:, GRID:]), axis=1)
    my_src = where_ref[4]
    keep = pltpu.make_async_copy(resist_ref.at[pl.ds(my_src * ROWS, ROWS)], resist_hbm, sems.at[1])
    keep.start()
    adjoint4 = dot(grid_yt_ref[...], fold_ref[...])
    adjoint2 = adjoint4[:GRID] + adjoint4[GRID:]
    coarse_adjoint = 2.0 * (adjoint2[:, :GRID] + adjoint2[:, GRID:])
    grad_ref[...] = jnp.zeros(grad_ref.shape, jnp.float32)
    for source in range(SOURCES):
        shift_a = ints_ref[source, 0]
        shift_b = ints_ref[source, 1]
        weight = ints_ref[source, 2].astype(jnp.float32) * (1.0 / (4.0 * SOURCES))
        weighted = weight * coarse_adjoint
        dfield_h, dfield_l = halves(field_ref[source] * jnp.concatenate([weighted, weighted], axis=1))
        dline2 = dot(dfield_h, right_t_ref[...])
        dline = dline2[:, :128] + dline2[:, 128:] + dot(dfield_l, right_t_ref[:, :128])
        damp4 = dot(left_t_ref[...], jnp.concatenate(halves(dline), axis=1))
        damp2 = damp4[:128] + damp4[128:]
        damp1 = damp2[:, :128] + damp2[:, 128:]
        swapped = pltpu.roll(damp1[64:], 64, 1)
        damp = damp1[:64] + jnp.where(low_w, swapped, -swapped)
        grad = pupil_ref[0] * damp - pupil_ref[1] * pltpu.roll(damp, 64, 1)
        rows = pl.ds(32 - shift_a, 64)
        grad_ref[0, rows, :] += pltpu.roll(jnp.where(low_w, grad, 0.0), 32 - shift_b, 1)
        grad_ref[1, rows, :] += pltpu.roll(jnp.where(low_w, 0.0, grad), lax.rem(96 - shift_b, 128), 1)
    grads = jnp.concatenate([grad_ref[0], grad_ref[1]], axis=0)
    folded = dot(jnp.concatenate(halves(grads), axis=1), unfold_ref[2])
    fold_re, fold_im = folded[:FREQ], folded[FREQ:]
    packed = jnp.concatenate(
        [jnp.where(low, fold_re, -fold_im), jnp.where(low, -fold_im, -fold_re)], axis=0
    )
    tables = jnp.concatenate([edge_ref[...], mine_a_ref[...], mine_b_ref[...]], axis=0)
    back = jnp.dot(tables, packed, precision=lax.Precision.HIGHEST, preferred_element_type=jnp.float32)
    sent_ref[...] = jnp.zeros(sent_ref.shape, jnp.bfloat16)

    @pl.when(where_ref[6] > 0)
    def _():
        sent_ref[where_ref[5]] = back[:HALO].astype(jnp.bfloat16)

    back_ref[...] = back[HALO:]
    keep.wait()


def make_fields(where, ints, got, own, pupil, target):
    whole = pl.BlockSpec(memory_space=pltpu.VMEM)
    const = lambda table: jnp.asarray(table)
    grid_spec = pltpu.PrefetchScalarGridSpec(
        num_scalar_prefetch=2,
        grid=(1,),
        in_specs=[
            pl.BlockSpec((1, HALO, 128), lambda i, where, ints: (where[0], 0, 0)),
            pl.BlockSpec((1, HALO, 128), lambda i, where, ints: (where[1], 0, 0)),
        ]
        + [whole] * 11
        + [
            pl.BlockSpec((HALO, 2 * FREQ), lambda i, where, ints: (where[7], 0)),
            pl.BlockSpec((HALO, 2 * FREQ), lambda i, where, ints: (1 + 2 * where[4], 0)),
            pl.BlockSpec((HALO, 2 * FREQ), lambda i, where, ints: (2 + 2 * where[4], 0)),
            pl.BlockSpec(memory_space=pl.ANY),
        ],
        out_specs=[pl.BlockSpec(memory_space=pl.ANY), whole, whole],
        scratch_shapes=[
            pltpu.VMEM((TILE_PX, TILE_PX), jnp.bfloat16),
            pltpu.VMEM((TILE_PX, TILE_PX), jnp.float32),
            pltpu.VMEM((2, FREQ, FREQ), jnp.float32),
            pltpu.VMEM((SOURCES, GRID, 2 * GRID), jnp.float32),
            pltpu.VMEM((TILE_PX, 2 * GRID), jnp.bfloat16),
            pltpu.VMEM((2, FREQ, FREQ), jnp.float32),
            pltpu.SemaphoreType.DMA((2,)),
        ],
    )
    row_table = const(ROW_F32)
    return pl.pallas_call(
        fields_kernel,
        out_shape=(
            jax.ShapeDtypeStruct((ROWS, TILE_PX), jnp.float32),
            jax.ShapeDtypeStruct((ROWS, 128), jnp.float32),
            jax.ShapeDtypeStruct((32, HALO, 128), jnp.bfloat16),
        ),
        grid_spec=grid_spec,
        compiler_params=pltpu.CompilerParams(vmem_limit_bytes=48 * 1024 * 1024),
        interpret=INTERPRET,
        name="fields",
    )(
        where, ints, got, got, own, pupil, const(RIM_HL), const(UNFOLD), const(LEFT), const(RIGHT), const(RIGHT_T),
        const(LEFT_T), const(GRID_Y), const(GRID_YT), const(GRID_X), row_table, row_table, row_table, target,
    )


def steps_kernel(where_ref, got_ref, back_ref, col_ref, out_ref):
    rim = got_ref[0].astype(jnp.float32)
    top = jnp.where(where_ref[9] > 0, rim, 0.0)
    bottom = jnp.where(where_ref[10] > 0, rim, 0.0)
    back = -LEARN_RATE * (back_ref[...] + jnp.concatenate([top, bottom], axis=0))
    high, low = halves(back)
    out_ref[...] = dot_t(high, col_ref[...]) + dot_t(low, col_ref[...])


def make_steps(where, got, back, col):
    whole = pl.BlockSpec(memory_space=pltpu.VMEM)
    grid_spec = pltpu.PrefetchScalarGridSpec(
        num_scalar_prefetch=1,
        grid=(1,),
        in_specs=[pl.BlockSpec((1, HALO, 128), lambda i, where: (where[8], 0, 0)), whole, whole],
        out_specs=whole,
    )
    return pl.pallas_call(
        steps_kernel,
        out_shape=jax.ShapeDtypeStruct((ROWS, TILE_PX), jnp.float32),
        grid_spec=grid_spec,
        interpret=INTERPRET,
        name="steps",
    )(where, got, back, col)


def places(slot_pos, my_slot, my_src, src_count):
    slot_ids = jnp.arange(slot_pos.shape[0], dtype=jnp.int32)
    my_position = jnp.sum(jnp.where(slot_ids == my_slot, slot_pos, 0))
    above = jnp.sum(jnp.where(slot_pos == my_position - 1, slot_ids, 0))
    below = jnp.sum(jnp.where(slot_pos == my_position + 1, slot_ids, 0))
    has_above = my_position > 0
    has_below = my_position < slot_pos.shape[0] - 1
    first = my_src == 0
    last = my_src == src_count - 1
    return jnp.stack(
        [
            above,
            below,
            has_above.astype(jnp.int32),
            has_below.astype(jnp.int32),
            my_src,
            jnp.where(first, below, above),
            jnp.where(first, has_below, has_above).astype(jnp.int32),
            jnp.where(first, (EXT_PX - HALO) // HALO, 0),
            jnp.where(first, above, below),
            (first & has_above).astype(jnp.int32),
            (last & has_below).astype(jnp.int32),
        ]
    ).astype(jnp.int32)


def pupil_tables(pupil_phase):
    window = pupil_phase[32:96, 32:96]
    real = jnp.where(DISC, jnp.cos(window), 0.0) * SCALE
    imag = jnp.where(DISC, jnp.sin(window), 0.0) * SCALE
    return jnp.stack([jnp.concatenate([real, real], axis=1), jnp.concatenate([-imag, imag], axis=1)])


def own_half(tile, col):
    half = jnp.dot(tile, col, preferred_element_type=jnp.float32)
    rows = jnp.asarray(ROW_F32[HALO : HALO + TILE_PX])
    return lax.dot_general(
        rows, half, (((0,), (0,)), ((), ())), precision=lax.Precision.HIGHEST, preferred_element_type=jnp.float32
    )


def per_device(mask_tiles, slot_pos, src_shift, src_weight, pupil_phase, target):
    src_count = lax.axis_size("src")
    where = places(slot_pos, lax.axis_index("tile"), lax.axis_index("src"), src_count)
    ints = jnp.concatenate([src_shift, src_weight[:, None]], axis=1)
    step = 1
    while step < src_count:
        other = lax.ppermute(ints, "src", [(i, i ^ step) for i in range(src_count)])
        ints = jnp.concatenate([ints, other], axis=0)
        step *= 2
    col = jnp.asarray(COL)
    tile = mask_tiles[0]
    got = lax.all_to_all(make_rims(where, tile, col), "tile", 0, 0, tiled=True)
    resist, back, sent = make_fields(where, ints, got, own_half(tile, col), pupil_tables(pupil_phase), target[0])
    got = lax.all_to_all(sent, "tile", 0, 0, tiled=True)
    return (resist[None], make_steps(where, got, back, col)[None])


def solution(mesh):
    return jax.shard_map(
        per_device,
        mesh=mesh,
        in_specs=(P("tile", None, None), P(), P("src", None), P("src"), P(), P("tile", None, None)),
        out_specs=(P("tile", "src", None), P("tile", "src", None)),
        check_vma=False,
    )
```

```python
import math

import jax
import jax.numpy as jnp
import ml_dtypes
import numpy as np
from jax import lax
from jax.experimental import pallas as pl
from jax.experimental.pallas import tpu as pltpu
from jax.sharding import PartitionSpec as P

TILE_PX = 1024
HALO = 64
EXT_PX = 1152
FREQ = 128
GRID = 128
SOURCES = 16
TILES = 32
SRC_DEVICES = 8
PUPIL_R = 28
ROWS = 128
STEEPNESS = 4.0
THRESHOLD = 0.6
LEARN_RATE = 8.0
SCALE = 1.0 / (FREQ / 2 * math.sqrt(EXT_PX * TILE_PX))
INTERPRET = False
BF16 = ml_dtypes.bfloat16


def split(table):
    high = table.astype(BF16)
    return high, (table - high.astype(np.float64)).astype(BF16)


def half_table(count, period):
    angle = 2 * np.pi * ((np.arange(count)[:, None] * np.arange(64)[None]) % period) / period
    return np.concatenate([np.cos(angle), np.sin(angle)], axis=1)


def unfold_tables():
    even = np.zeros((FREQ, 64))
    odd = np.zeros((FREQ, 64))
    for row, freq in enumerate(range(-64, 64)):
        if freq > -64:
            even[row, abs(freq)] = 1
            odd[row, abs(freq)] = np.sign(freq)
    return even, odd


def coarse_table():
    angle = 2 * np.pi * ((np.arange(GRID)[:, None] * (np.arange(64) - 32)[None]) % GRID) / GRID
    return np.cos(angle), np.sin(angle)


def interpolation(positions):
    apart = positions[:, None] - np.arange(GRID)[None]
    return np.cos(2 * np.pi * apart[:, :, None] * np.arange(-63, 64) / GRID).sum(axis=-1) / GRID


COL = half_table(TILE_PX, TILE_PX).astype(BF16)
ROW = half_table(EXT_PX, EXT_PX)
EVEN, ODD = unfold_tables()
COS_W, SIN_W = coarse_table()
ROW_F32 = ROW.astype(np.float32)
ZERO = np.zeros((FREQ, 64))
UNFOLD = np.concatenate(
    [np.concatenate([EVEN, ZERO], axis=1), np.concatenate([ZERO, ODD], axis=1)], axis=0
)
LEFT_H, LEFT_L = split(np.concatenate([COS_W, SIN_W], axis=0))
RIGHT = np.concatenate(
    split(
        np.concatenate(
            [np.concatenate([COS_W.T, SIN_W.T], axis=1), np.concatenate([-SIN_W.T, COS_W.T], axis=1)], axis=0
        )
    ),
    axis=0,
)
LEFT_T = np.concatenate(split(np.concatenate([COS_W.T, SIN_W.T], axis=0)), axis=0)
RIM = np.concatenate(split(np.concatenate([ROW[:HALO], ROW[EXT_PX - HALO :]], axis=0).T), axis=1)
LANES = np.concatenate([EVEN, ODD], axis=1)
SMALL = np.concatenate(
    [
        UNFOLD.astype(BF16),
        np.concatenate([LEFT_H, LEFT_H, LEFT_L, np.zeros_like(LEFT_L)], axis=1),
        RIGHT,
        LEFT_T,
        np.concatenate([RIM, UNFOLD.T.astype(BF16)], axis=0),
        np.concatenate([LANES, np.zeros_like(LANES)], axis=0).astype(BF16),
    ],
    axis=1,
)
ROWS_Y = (HALO + np.arange(TILE_PX)) / 9.0
GRIDS = np.concatenate(split(interpolation(ROWS_Y)) + split(interpolation(np.arange(TILE_PX) / 8.0)), axis=1)
GRID_YT = np.concatenate(split(interpolation(ROWS_Y).T), axis=0)
DISC = (np.arange(64)[:, None] - 32) ** 2 + (np.arange(64)[None] - 32) ** 2 <= PUPIL_R * PUPIL_R


def dot(left, right):
    return jnp.dot(left, right, preferred_element_type=jnp.float32)


def dot_t(left, right):
    return lax.dot_general(left, right, (((1,), (1,)), ((), ())), preferred_element_type=jnp.float32)


def halves(value):
    high = value.astype(jnp.bfloat16)
    return high, (value - high.astype(jnp.float32)).astype(jnp.bfloat16)


def low_lanes(shape):
    return lax.broadcasted_iota(jnp.int32, shape, 1) < 64


def places(slot_ref):
    my_slot = lax.axis_index("tile")
    my_position = slot_ref[my_slot]
    above = jnp.int32(-1)
    below = jnp.int32(-1)
    for slot in range(TILES):
        position = slot_ref[slot]
        above = jnp.where(position == my_position - 1, slot, above)
        below = jnp.where(position == my_position + 1, slot, below)
    return my_slot, lax.axis_index("src"), above, below


def rims_kernel(slot_ref, tile_ref, col_ref, sent_ref, rows_ref, sems):
    copies = [
        pltpu.make_async_copy(tile_ref.at[pl.ds(start, HALO)], rows_ref.at[pl.ds(place, HALO)], sems.at[number])
        for number, (start, place) in enumerate(((0, 0), (TILE_PX - HALO, HALO)))
    ]
    for copy in copies:
        copy.start()
    my_slot, my_src, above, below = places(slot_ref)
    sent_ref[...] = jnp.zeros(sent_ref.shape, jnp.bfloat16)
    for copy in copies:
        copy.wait()
    rims = dot(rows_ref[...], col_ref[...]).astype(jnp.bfloat16)

    @pl.when(above >= 0)
    def _():
        sent_ref[above] = rims[:HALO]

    @pl.when(below >= 0)
    def _():
        sent_ref[below] = rims[HALO:]


SCALARS = pl.BlockSpec(memory_space=pltpu.SMEM)
WHOLE = pl.BlockSpec(memory_space=pltpu.VMEM)
LEFT_THERE = pl.BlockSpec(memory_space=pl.ANY)


def make_rims(slot_pos, tile, col):
    return pl.pallas_call(
        rims_kernel,
        out_shape=jax.ShapeDtypeStruct((TILES, HALO, 128), jnp.bfloat16),
        in_specs=[SCALARS, LEFT_THERE, WHOLE],
        out_specs=WHOLE,
        scratch_shapes=[pltpu.VMEM((2 * HALO, TILE_PX), jnp.bfloat16), pltpu.SemaphoreType.DMA((2,))],
        interpret=INTERPRET,
        name="rims",
    )(slot_pos, tile, col)


def fields_kernel(
    slot_ref, ints_ref, got_ref, own_ref, pupil_ref, small_ref, grids_ref, grid_yt_ref, row_ref, target_hbm,
    resist_hbm, back_ref, sent_ref,
    target_ref, resist_ref, spec_ref, field_ref, fold_ref, grad_ref, sems,
):
    fetch = pltpu.make_async_copy(target_hbm, target_ref, sems.at[0])
    fetch.start()
    my_slot, my_src, above, below = places(slot_ref)
    unfold = small_ref[:, 0:128]
    left = small_ref[:, 128:320]
    right = small_ref[:, 384:640]
    left_t = small_ref[:, 640:768]
    rim_table = small_ref[:128, 768:1024]
    unfold_t = small_ref[128:, 768:1024]
    lanes = small_ref[:128, 1024:1152]
    lanes2 = jnp.concatenate([lanes, lanes], axis=1)
    low = low_lanes((128, 128))
    low_w = low_lanes((64, 128))
    up = jnp.where(above >= 0, got_ref[jnp.maximum(above, 0)].astype(jnp.float32), 0.0)
    down = jnp.where(below >= 0, got_ref[jnp.maximum(below, 0)].astype(jnp.float32), 0.0)
    rims = jnp.concatenate([up, down], axis=0).astype(jnp.bfloat16)
    moments = own_ref[...] + dot(rim_table, jnp.concatenate([rims, rims], axis=0))
    half = dot(jnp.concatenate([unfold, unfold], axis=1), jnp.concatenate(halves(moments), axis=0))
    by_cos, by_sin = half[:FREQ], half[FREQ:]
    spec_ref[0] = dot_t(jnp.concatenate(halves(jnp.where(low, by_cos, -by_sin)), axis=1), lanes2)
    spec_ref[1] = dot_t(jnp.concatenate(halves(jnp.where(low, -by_sin, -by_cos)), axis=1), lanes2)
    coarse = jnp.zeros((GRID, GRID), jnp.float32)
    for source in range(SOURCES):
        shift_a = ints_ref[source, 0]
        shift_b = ints_ref[source, 1]
        rows = pl.ds(32 - shift_a, 64)
        spec_re = spec_ref[0, rows, :]
        spec_im = spec_ref[1, rows, :]
        near = lax.rem(96 + shift_b, 128)
        far = 32 + shift_b
        window = jnp.where(low_w, pltpu.roll(spec_re, near, 1), pltpu.roll(spec_im, far, 1))
        amp = pupil_ref[0] * window + pupil_ref[1] * pltpu.roll(window, 64, 1)
        amp_h, amp_l = halves(amp)
        both = dot(left, jnp.concatenate([amp_h, amp_l, amp_h], axis=0))
        swapped = pltpu.roll(both[GRID:], 64, 1)
        line = both[:GRID] + jnp.where(low, -swapped, swapped)
        line_h, line_l = halves(line)
        field = dot(jnp.concatenate([line_h, line_h], axis=1), right) + dot(line_l, right[:128])
        field_ref[source] = field
        weight = ints_ref[source, 2].astype(jnp.float32) * (1.0 / (4.0 * SOURCES))
        squared = field * field
        coarse = coarse + weight * (squared[:, :GRID] + squared[:, GRID:])
    coarse_h, coarse_l = halves(coarse)
    coarse_hh = jnp.concatenate([coarse_h, coarse_h], axis=0)
    grid_x = grids_ref[:, 256:512]
    fetch.wait()
    chunk = 256
    for place in range(TILE_PX // chunk):
        rows = pl.ds(place * chunk, chunk)
        rows_y = dot(grids_ref[rows, 0:256], coarse_hh) + dot(grids_ref[rows, 0:128], coarse_l)
        rows_h, rows_l = halves(rows_y)
        intensity = dot_t(jnp.concatenate([rows_h, rows_h], axis=1), grid_x) + dot_t(rows_l, grid_x[:, :GRID])
        resist = jax.nn.sigmoid(STEEPNESS * (intensity - THRESHOLD))
        resist_ref[rows, :] = resist
        wanted = target_ref[rows, :].astype(jnp.float32)
        adjoint = ((2.0 * STEEPNESS) * (resist - wanted) * resist * (1.0 - resist)).astype(jnp.bfloat16)
        folded = dot(adjoint, grid_x)
        fold_ref[rows, :] = jnp.concatenate(halves(folded[:, :GRID] + folded[:, GRID:]), axis=1)
    mine = pl.multiple_of(my_src * ROWS, ROWS)
    keep = pltpu.make_async_copy(resist_ref.at[pl.ds(mine, ROWS)], resist_hbm, sems.at[1])
    keep.start()
    adjoint4 = dot(grid_yt_ref[...], fold_ref[...])
    adjoint2 = adjoint4[:GRID] + adjoint4[GRID:]
    coarse_adjoint = 2.0 * (adjoint2[:, :GRID] + adjoint2[:, GRID:])
    grad_ref[...] = jnp.zeros(grad_ref.shape, jnp.float32)
    for source in range(SOURCES):
        shift_a = ints_ref[source, 0]
        shift_b = ints_ref[source, 1]
        weight = ints_ref[source, 2].astype(jnp.float32) * (1.0 / (4.0 * SOURCES))
        weighted = weight * coarse_adjoint
        dfield_h, dfield_l = halves(field_ref[source] * jnp.concatenate([weighted, weighted], axis=1))
        dline2 = dot_t(dfield_h, right)
        dline = dline2[:, :128] + dline2[:, 128:] + dot_t(dfield_l, right[:128])
        damp4 = dot(left_t, jnp.concatenate(halves(dline), axis=1))
        damp2 = damp4[:128] + damp4[128:]
        damp1 = damp2[:, :128] + damp2[:, 128:]
        swapped = pltpu.roll(damp1[64:], 64, 1)
        damp = damp1[:64] + jnp.where(low_w, swapped, -swapped)
        grad = pupil_ref[0] * damp - pupil_ref[1] * pltpu.roll(damp, 64, 1)
        rows = pl.ds(32 - shift_a, 64)
        grad_ref[0, rows, :] += pltpu.roll(jnp.where(low_w, grad, 0.0), 32 - shift_b, 1)
        grad_ref[1, rows, :] += pltpu.roll(jnp.where(low_w, 0.0, grad), lax.rem(96 - shift_b, 128), 1)
    grads = jnp.concatenate([grad_ref[0], grad_ref[1]], axis=0)
    folded = dot(jnp.concatenate(halves(grads), axis=1), jnp.concatenate([lanes, lanes], axis=0))
    fold_re, fold_im = folded[:FREQ], folded[FREQ:]
    packed = jnp.concatenate(
        [jnp.where(low, fold_re, -fold_im), jnp.where(low, -fold_im, -fold_re)], axis=0
    )
    packed = dot(jnp.concatenate([unfold_t, unfold_t], axis=1), jnp.concatenate(halves(packed), axis=0))
    first = my_src == 0
    edge_rows = row_ref[pl.ds(pl.multiple_of(jnp.where(first, EXT_PX - HALO, 0), HALO), HALO), :]
    mine_rows = row_ref[pl.ds(pl.multiple_of(HALO + my_src * ROWS, HALO), ROWS), :]
    tables = jnp.concatenate([edge_rows, mine_rows], axis=0)
    back = jnp.dot(tables, packed, precision=lax.Precision.HIGHEST, preferred_element_type=jnp.float32)
    sent_ref[...] = jnp.zeros(sent_ref.shape, jnp.bfloat16)
    goes_to = jnp.where(first, below, above)

    @pl.when(goes_to >= 0)
    def _():
        sent_ref[goes_to // 2] = back[:HALO].astype(jnp.bfloat16)

    back_ref[...] = back[HALO:]
    keep.wait()


def make_fields(slot_pos, ints, got, own, pupil, row_table, target):
    return pl.pallas_call(
        fields_kernel,
        out_shape=(
            jax.ShapeDtypeStruct((ROWS, TILE_PX), jnp.float32),
            jax.ShapeDtypeStruct((ROWS, 128), jnp.float32),
            jax.ShapeDtypeStruct((TILES // 2, HALO, 128), jnp.bfloat16),
        ),
        in_specs=[SCALARS, SCALARS] + [WHOLE] * 7 + [LEFT_THERE],
        out_specs=[LEFT_THERE, WHOLE, WHOLE],
        scratch_shapes=[
            pltpu.VMEM((TILE_PX, TILE_PX), jnp.bfloat16),
            pltpu.VMEM((TILE_PX, TILE_PX), jnp.float32),
            pltpu.VMEM((2, FREQ, FREQ), jnp.float32),
            pltpu.VMEM((SOURCES, GRID, 2 * GRID), jnp.float32),
            pltpu.VMEM((TILE_PX, 2 * GRID), jnp.bfloat16),
            pltpu.VMEM((2, FREQ, FREQ), jnp.float32),
            pltpu.SemaphoreType.DMA((2,)),
        ],
        compiler_params=pltpu.CompilerParams(vmem_limit_bytes=48 * 1024 * 1024),
        interpret=INTERPRET,
        name="fields",
    )(
        slot_pos, ints, got, own, pupil, jnp.asarray(SMALL), jnp.asarray(GRIDS), jnp.asarray(GRID_YT), row_table, target
    )


def steps_kernel(slot_ref, got_ref, other_ref, back_ref, col_ref, out_ref):
    my_slot, my_src, above, below = places(slot_ref)
    first = my_src == 0
    last = my_src == SRC_DEVICES - 1
    comes_from = jnp.where(first, above, below)
    place = jnp.maximum(comes_from, 0) // 2
    same_core = lax.rem(jnp.maximum(comes_from, 0), 2) == lax.rem(my_slot, 2)
    rim = jnp.where(same_core, got_ref[place].astype(jnp.float32), other_ref[place].astype(jnp.float32))
    top = jnp.where(first & (above >= 0), rim, 0.0)
    bottom = jnp.where(last & (below >= 0), rim, 0.0)
    back = -LEARN_RATE * (back_ref[...] + jnp.concatenate([top, bottom], axis=0))
    high, low = halves(back)
    out_ref[...] = dot_t(high, col_ref[...]) + dot_t(low, col_ref[...])


def make_steps(slot_pos, got, other, back, col):
    return pl.pallas_call(
        steps_kernel,
        out_shape=jax.ShapeDtypeStruct((ROWS, TILE_PX), jnp.float32),
        in_specs=[SCALARS] + [WHOLE] * 4,
        out_specs=WHOLE,
        interpret=INTERPRET,
        name="steps",
    )(slot_pos, got, other, back, col)


def pupil_tables(pupil_phase):
    window = pupil_phase[32:96, 32:96]
    real = jnp.where(DISC, jnp.cos(window), 0.0) * SCALE
    imag = jnp.where(DISC, jnp.sin(window), 0.0) * SCALE
    return jnp.stack([jnp.concatenate([real, real], axis=1), jnp.concatenate([-imag, imag], axis=1)])


def own_moments(tile, col, row_table):
    half = jnp.dot(tile, col, preferred_element_type=jnp.float32)
    rows = row_table[HALO : HALO + TILE_PX]
    return lax.dot_general(
        rows, half, (((0,), (0,)), ((), ())), precision=lax.Precision.HIGHEST, preferred_element_type=jnp.float32
    )


def all_sources(src_shift, src_weight):
    ints = jnp.concatenate([src_shift, src_weight[:, None]], axis=1)
    swap = lambda value, mask: lax.ppermute(value, "src", [(i, i ^ mask) for i in range(SRC_DEVICES)])
    near = jnp.concatenate([ints] + [swap(ints, mask) for mask in (1, 2, 3)], axis=0)
    return jnp.concatenate([near, swap(near, 4)], axis=0)


def per_device(mask_tiles, slot_pos, src_shift, src_weight, pupil_phase, target):
    ints = all_sources(src_shift, src_weight)
    col = jnp.asarray(COL)
    row_table = lax.optimization_barrier(jnp.asarray(ROW_F32))
    tile = mask_tiles[0]
    got = lax.all_to_all(make_rims(slot_pos, tile, col), "tile", 0, 0, tiled=True)
    own = own_moments(tile, col, row_table)
    resist, back, sent = make_fields(slot_pos, ints, got, own, pupil_tables(pupil_phase), row_table, target[0])
    cores = [[2 * chip + core for chip in range(TILES // 2)] for core in range(2)]
    got = lax.all_to_all(sent, "tile", 0, 0, tiled=True, axis_index_groups=cores)
    other = lax.ppermute(got, "tile", [(i, i ^ 1) for i in range(TILES)])
    return (resist[None], make_steps(slot_pos, got, other, back, col)[None])


def solution(mesh):
    return jax.shard_map(
        per_device,
        mesh=mesh,
        in_specs=(P("tile", None, None), P(), P("src", None), P("src"), P(), P("tile", None, None)),
        out_specs=(P("tile", "src", None), P("tile", "src", None)),
        check_vma=False,
    )
```

```python
import math

import jax
import jax.numpy as jnp
import ml_dtypes
import numpy as np
from jax import lax
from jax.experimental import pallas as pl
from jax.experimental.pallas import tpu as pltpu
from jax.sharding import PartitionSpec as P

TILE_PX = 1024
HALO = 64
EXT_PX = 1152
FREQ = 128
GRID = 128
SOURCES = 16
TILES = 32
SRC_DEVICES = 8
PUPIL_R = 28
ROWS = 128
STEEPNESS = 4.0
THRESHOLD = 0.6
LEARN_RATE = 8.0
SCALE = 1.0 / (FREQ / 2 * math.sqrt(EXT_PX * TILE_PX))
INTERPRET = False
BF16 = ml_dtypes.bfloat16


def split(table):
    high = table.astype(BF16)
    return high, (table - high.astype(np.float64)).astype(BF16)


def half_table(count, period):
    angle = 2 * np.pi * ((np.arange(count)[:, None] * np.arange(64)[None]) % period) / period
    return np.concatenate([np.cos(angle), np.sin(angle)], axis=1)


def unfold_tables():
    even = np.zeros((FREQ, 64))
    odd = np.zeros((FREQ, 64))
    for row, freq in enumerate(range(-64, 64)):
        if freq > -64:
            even[row, abs(freq)] = 1
            odd[row, abs(freq)] = np.sign(freq)
    return even, odd


def coarse_table():
    angle = 2 * np.pi * ((np.arange(GRID)[:, None] * (np.arange(64) - 32)[None]) % GRID) / GRID
    return np.cos(angle), np.sin(angle)


def interpolation(positions):
    apart = positions[:, None] - np.arange(GRID)[None]
    return np.cos(2 * np.pi * apart[:, :, None] * np.arange(-63, 64) / GRID).sum(axis=-1) / GRID


COL = half_table(TILE_PX, TILE_PX).astype(BF16)
ROW = half_table(EXT_PX, EXT_PX)
EVEN, ODD = unfold_tables()
COS_W, SIN_W = coarse_table()
ROW_F32 = ROW.astype(np.float32)
ZERO = np.zeros((FREQ, 64))
UNFOLD = np.concatenate(
    [np.concatenate([EVEN, ZERO], axis=1), np.concatenate([ZERO, ODD], axis=1)], axis=0
)
LEFT_H, LEFT_L = split(np.concatenate([COS_W, SIN_W], axis=0))
RIGHT = np.concatenate(
    split(
        np.concatenate(
            [np.concatenate([COS_W.T, SIN_W.T], axis=1), np.concatenate([-SIN_W.T, COS_W.T], axis=1)], axis=0
        )
    ),
    axis=0,
)
LEFT_T = np.concatenate(split(np.concatenate([COS_W.T, SIN_W.T], axis=0)), axis=0)
RIM = np.concatenate(split(np.concatenate([ROW[:HALO], ROW[EXT_PX - HALO :]], axis=0).T), axis=1)
LANES = np.concatenate([EVEN, ODD], axis=1)
SMALL = np.concatenate(
    [
        UNFOLD.astype(BF16),
        np.concatenate([LEFT_H, LEFT_H, LEFT_L, np.zeros_like(LEFT_L)], axis=1),
        RIGHT,
        LEFT_T,
        np.concatenate([RIM, UNFOLD.T.astype(BF16)], axis=0),
        np.concatenate([LANES, np.zeros_like(LANES)], axis=0).astype(BF16),
    ],
    axis=1,
)
ROWS_Y = (HALO + np.arange(TILE_PX)) / 9.0
GRIDS = np.concatenate(split(interpolation(ROWS_Y)) + split(interpolation(np.arange(TILE_PX) / 8.0)), axis=1)
DISC = (np.arange(64)[:, None] - 32) ** 2 + (np.arange(64)[None] - 32) ** 2 <= PUPIL_R * PUPIL_R


def dot(left, right):
    return jnp.dot(left, right, preferred_element_type=jnp.float32)


def dot_t(left, right):
    return lax.dot_general(left, right, (((1,), (1,)), ((), ())), preferred_element_type=jnp.float32)


def halves(value):
    high = value.astype(jnp.bfloat16)
    return high, (value - high.astype(jnp.float32)).astype(jnp.bfloat16)


def low_lanes(shape):
    return lax.broadcasted_iota(jnp.int32, shape, 1) < 64


def places(slot_ref):
    my_slot = lax.axis_index("tile")
    my_position = slot_ref[my_slot]
    above = jnp.int32(-1)
    below = jnp.int32(-1)
    for slot in range(TILES):
        position = slot_ref[slot]
        above = jnp.where(position == my_position - 1, slot, above)
        below = jnp.where(position == my_position + 1, slot, below)
    return my_slot, lax.axis_index("src"), above, below


def rims_kernel(slot_ref, tile_hbm, col_hbm, sent_hbm, rows_ref, col_ref, rims_ref, sems):
    copies = [
        pltpu.make_async_copy(col_hbm, col_ref, sems.at[0]),
        pltpu.make_async_copy(tile_hbm.at[pl.ds(0, HALO)], rows_ref.at[pl.ds(0, HALO)], sems.at[1]),
        pltpu.make_async_copy(
            tile_hbm.at[pl.ds(TILE_PX - HALO, HALO)], rows_ref.at[pl.ds(HALO, HALO)], sems.at[2]
        ),
    ]
    for copy in copies:
        copy.start()
    my_slot, my_src, above, below = places(slot_ref)
    for copy in copies:
        copy.wait()
    rims_ref[...] = dot(rows_ref[...], col_ref[...]).astype(jnp.bfloat16).reshape(2, HALO, 128)

    for number, slot in enumerate((above, below)):

        @pl.when(slot >= 0)
        def _():
            pltpu.make_async_copy(rims_ref.at[number], sent_hbm.at[slot], sems.at[3 + number]).start()

    for number, slot in enumerate((above, below)):

        @pl.when(slot >= 0)
        def _():
            pltpu.make_async_copy(rims_ref.at[number], sent_hbm.at[slot], sems.at[3 + number]).wait()


SCALARS = pl.BlockSpec(memory_space=pltpu.SMEM)
WHOLE = pl.BlockSpec(memory_space=pltpu.VMEM)
LEFT_THERE = pl.BlockSpec(memory_space=pltpu.MemorySpace.HBM)
MIB = 1024 * 1024
ALL_VMEM = 63_000_000


def make_rims(slot_pos, tile, col):
    return pl.pallas_call(
        rims_kernel,
        out_shape=jax.ShapeDtypeStruct((TILES, HALO, 128), jnp.bfloat16),
        in_specs=[SCALARS, LEFT_THERE, LEFT_THERE],
        out_specs=LEFT_THERE,
        scratch_shapes=[
            pltpu.VMEM((2 * HALO, TILE_PX), jnp.bfloat16),
            pltpu.VMEM((TILE_PX, 128), jnp.bfloat16),
            pltpu.VMEM((2, HALO, 128), jnp.bfloat16),
            pltpu.SemaphoreType.DMA((5,)),
        ],
        compiler_params=pltpu.CompilerParams(vmem_limit_bytes=ALL_VMEM),
        interpret=INTERPRET,
        name="rims",
    )(slot_pos, tile, col)


def prep_kernel(small_hbm, grids_hbm, flipped_hbm, right_t_hbm, small_ref, grids_ref, flipped_ref, right_t_ref, sems):
    fetches = [
        pltpu.make_async_copy(grids_hbm, grids_ref, sems.at[0]),
        pltpu.make_async_copy(small_hbm.at[:, pl.ds(384, 256)], small_ref, sems.at[1]),
    ]
    keeps = [
        pltpu.make_async_copy(flipped_ref, flipped_hbm, sems.at[2]),
        pltpu.make_async_copy(right_t_ref, right_t_hbm, sems.at[3]),
    ]
    for fetch in fetches:
        fetch.start()
    fetches[0].wait()
    flipped_ref[...] = grids_ref[...].T
    keeps[0].start()
    fetches[1].wait()
    right_t_ref[...] = small_ref[...].T
    keeps[1].start()
    for keep in keeps:
        keep.wait()


def flip_tables(small, grids):
    return pl.pallas_call(
        prep_kernel,
        out_shape=(
            jax.ShapeDtypeStruct(GRIDS.shape[::-1], jnp.bfloat16),
            jax.ShapeDtypeStruct((256, 256), jnp.bfloat16),
        ),
        in_specs=[LEFT_THERE] * 2,
        out_specs=[LEFT_THERE] * 2,
        scratch_shapes=[
            pltpu.VMEM((256, 256), jnp.bfloat16),
            pltpu.VMEM(GRIDS.shape, jnp.bfloat16),
            pltpu.VMEM(GRIDS.shape[::-1], jnp.bfloat16),
            pltpu.VMEM((256, 256), jnp.bfloat16),
            pltpu.SemaphoreType.DMA((4,)),
        ],
        compiler_params=pltpu.CompilerParams(vmem_limit_bytes=ALL_VMEM),
        interpret=INTERPRET,
        name="prep",
    )(small, grids)


def fields_kernel(
    slot_ref, ints_ref, got_hbm, own_hbm, pupil_hbm, small_hbm, right_t_hbm, grids_hbm, flipped_hbm, row_hbm, target_hbm,
    resist_hbm, back_hbm, sent_hbm,
    got_ref, own_ref, pupil_ref, small_ref, right_t_ref, grids_ref, flipped_ref, row_ref, target_ref,
    back_ref, edge_ref, resist_ref, spec_ref, field_ref, fold_ref, grad_ref, sems,
):
    first_fetches = [
        pltpu.make_async_copy(source, target, sems.at[number])
        for number, (source, target) in enumerate(((small_hbm, small_ref), (own_hbm, own_ref), (pupil_hbm, pupil_ref)))
    ]
    for fetch in first_fetches:
        fetch.start()
    my_slot, my_src, above, below = places(slot_ref)
    for number, slot in enumerate((above, below)):
        first_fetches.append(
            pltpu.make_async_copy(got_hbm.at[jnp.maximum(slot, 0)], got_ref.at[number], sems.at[3 + number])
        )
        first_fetches[-1].start()
    fetches = [
        pltpu.make_async_copy(source, target, sems.at[5 + number])
        for number, (source, target) in enumerate(
            (
                (grids_hbm, grids_ref),
                (flipped_hbm, flipped_ref),
                (target_hbm, target_ref),
                (right_t_hbm, right_t_ref),
                (row_hbm, row_ref),
            )
        )
    ]
    for fetch in fetches:
        fetch.start()
    for fetch in first_fetches:
        fetch.wait()
    unfold = small_ref[:, 0:128]
    left = small_ref[:, 128:320]
    right = small_ref[:, 384:640]
    left_t = small_ref[:, 640:768]
    rim_table = small_ref[:128, 768:1024]
    unfold_t = small_ref[128:, 768:1024]
    lanes = small_ref[:128, 1024:1152]
    lanes2 = jnp.concatenate([lanes, lanes], axis=1)
    low = low_lanes((128, 128))
    low_w = low_lanes((64, 128))
    up = jnp.where(above >= 0, got_ref[0].astype(jnp.float32), 0.0)
    down = jnp.where(below >= 0, got_ref[1].astype(jnp.float32), 0.0)
    rims = jnp.concatenate([up, down], axis=0).astype(jnp.bfloat16)
    moments = own_ref[...] + dot(rim_table, jnp.concatenate([rims, rims], axis=0))
    half = dot(jnp.concatenate([unfold, unfold], axis=1), jnp.concatenate(halves(moments), axis=0))
    by_cos, by_sin = half[:FREQ], half[FREQ:]
    spec_ref[0] = dot_t(jnp.concatenate(halves(jnp.where(low, by_cos, -by_sin)), axis=1), lanes2)
    spec_ref[1] = dot_t(jnp.concatenate(halves(jnp.where(low, -by_sin, -by_cos)), axis=1), lanes2)
    coarse = jnp.zeros((GRID, GRID), jnp.float32)
    for source in range(SOURCES):
        shift_a = ints_ref[source, 0]
        shift_b = ints_ref[source, 1]
        rows = pl.ds(32 - shift_a, 64)
        spec_re = spec_ref[0, rows, :]
        spec_im = spec_ref[1, rows, :]
        near = lax.rem(96 + shift_b, 128)
        far = 32 + shift_b
        window = jnp.where(low_w, pltpu.roll(spec_re, near, 1), pltpu.roll(spec_im, far, 1))
        amp = pupil_ref[0] * window + pupil_ref[1] * pltpu.roll(window, 64, 1)
        amp_h, amp_l = halves(amp)
        both = dot(left, jnp.concatenate([amp_h, amp_l, amp_h], axis=0))
        swapped = pltpu.roll(both[GRID:], 64, 1)
        line = both[:GRID] + jnp.where(low, -swapped, swapped)
        line_h, line_l = halves(line)
        field = dot(jnp.concatenate([line_h, line_h], axis=1), right) + dot(line_l, right[:128])
        field_ref[source] = field
        weight = ints_ref[source, 2].astype(jnp.float32) * (1.0 / (4.0 * SOURCES))
        squared = field * field
        coarse = coarse + weight * (squared[:, :GRID] + squared[:, GRID:])
    coarse_h, coarse_l = halves(coarse)
    coarse_hh = jnp.concatenate([coarse_h, coarse_h], axis=0)
    for fetch in fetches[:3]:
        fetch.wait()
    grid_x = grids_ref[:, 256:512]
    grid_xt = flipped_ref[256:512, :]
    grid_yt = flipped_ref[0:256, :]
    chunk = 256
    for place in range(TILE_PX // chunk):
        rows = pl.ds(place * chunk, chunk)
        rows_y = dot(grids_ref[rows, 0:256], coarse_hh) + dot(grids_ref[rows, 0:128], coarse_l)
        rows_h, rows_l = halves(rows_y)
        intensity = dot(jnp.concatenate([rows_h, rows_h], axis=1), grid_xt) + dot(rows_l, grid_xt[:GRID])
        resist = jax.nn.sigmoid(STEEPNESS * (intensity - THRESHOLD))
        resist_ref[rows, :] = resist
        wanted = target_ref[rows, :].astype(jnp.float32)
        adjoint = ((2.0 * STEEPNESS) * (resist - wanted) * resist * (1.0 - resist)).astype(jnp.bfloat16)
        folded = dot(adjoint, grid_x)
        fold_ref[rows, :] = jnp.concatenate(halves(folded[:, :GRID] + folded[:, GRID:]), axis=1)
    mine = pl.multiple_of(my_src * ROWS, ROWS)
    keep = pltpu.make_async_copy(resist_ref.at[pl.ds(mine, ROWS)], resist_hbm, sems.at[10])
    keep.start()
    adjoint4 = dot(grid_yt, fold_ref[...])
    adjoint2 = adjoint4[:GRID] + adjoint4[GRID:]
    coarse_adjoint = 2.0 * (adjoint2[:, :GRID] + adjoint2[:, GRID:])
    fetches[3].wait()
    right_t = right_t_ref[...]
    grad_ref[...] = jnp.zeros(grad_ref.shape, jnp.float32)
    for source in range(SOURCES):
        shift_a = ints_ref[source, 0]
        shift_b = ints_ref[source, 1]
        weight = ints_ref[source, 2].astype(jnp.float32) * (1.0 / (4.0 * SOURCES))
        weighted = weight * coarse_adjoint
        dfield_h, dfield_l = halves(field_ref[source] * jnp.concatenate([weighted, weighted], axis=1))
        dline2 = dot(dfield_h, right_t)
        dline = dline2[:, :128] + dline2[:, 128:] + dot(dfield_l, right_t[:, :128])
        damp4 = dot(left_t, jnp.concatenate(halves(dline), axis=1))
        damp2 = damp4[:128] + damp4[128:]
        damp1 = damp2[:, :128] + damp2[:, 128:]
        swapped = pltpu.roll(damp1[64:], 64, 1)
        damp = damp1[:64] + jnp.where(low_w, swapped, -swapped)
        grad = pupil_ref[0] * damp - pupil_ref[1] * pltpu.roll(damp, 64, 1)
        rows = pl.ds(32 - shift_a, 64)
        grad_ref[0, rows, :] += pltpu.roll(jnp.where(low_w, grad, 0.0), 32 - shift_b, 1)
        grad_ref[1, rows, :] += pltpu.roll(jnp.where(low_w, 0.0, grad), lax.rem(96 - shift_b, 128), 1)
    grads = jnp.concatenate([grad_ref[0], grad_ref[1]], axis=0)
    folded = dot(jnp.concatenate(halves(grads), axis=1), jnp.concatenate([lanes, lanes], axis=0))
    fold_re, fold_im = folded[:FREQ], folded[FREQ:]
    packed = jnp.concatenate(
        [jnp.where(low, fold_re, -fold_im), jnp.where(low, -fold_im, -fold_re)], axis=0
    )
    packed = dot(jnp.concatenate([unfold_t, unfold_t], axis=1), jnp.concatenate(halves(packed), axis=0))
    fetches[4].wait()
    first = my_src == 0
    edge_rows = row_ref[pl.ds(pl.multiple_of(jnp.where(first, EXT_PX - HALO, 0), HALO), HALO), :]
    mine_rows = row_ref[pl.ds(pl.multiple_of(HALO + my_src * ROWS, HALO), ROWS), :]
    tables = jnp.concatenate([edge_rows, mine_rows], axis=0)
    back = jnp.dot(tables, packed, precision=lax.Precision.HIGHEST, preferred_element_type=jnp.float32)
    goes_to = jnp.where(first, below, above)
    edge_ref[...] = back[:HALO].astype(jnp.bfloat16)
    back_ref[...] = back[HALO:]
    back_keep = pltpu.make_async_copy(back_ref, back_hbm, sems.at[11])
    back_keep.start()

    @pl.when(goes_to >= 0)
    def _():
        send = pltpu.make_async_copy(edge_ref, sent_hbm.at[goes_to // 2], sems.at[12])
        send.start()
        send.wait()

    back_keep.wait()
    keep.wait()


def make_fields(slot_pos, ints, *arrays):
    return pl.pallas_call(
        fields_kernel,
        out_shape=(
            jax.ShapeDtypeStruct((ROWS, TILE_PX), jnp.float32),
            jax.ShapeDtypeStruct((ROWS, 128), jnp.float32),
            jax.ShapeDtypeStruct((TILES // 2, HALO, 128), jnp.bfloat16),
        ),
        in_specs=[SCALARS, SCALARS] + [LEFT_THERE] * 9,
        out_specs=[LEFT_THERE] * 3,
        scratch_shapes=[
            pltpu.VMEM((2, HALO, 128), jnp.bfloat16),
            pltpu.VMEM((128, 128), jnp.float32),
            pltpu.VMEM((2, 64, 128), jnp.float32),
            pltpu.VMEM(SMALL.shape, jnp.bfloat16),
            pltpu.VMEM((256, 256), jnp.bfloat16),
            pltpu.VMEM(GRIDS.shape, jnp.bfloat16),
            pltpu.VMEM(GRIDS.shape[::-1], jnp.bfloat16),
            pltpu.VMEM(ROW_F32.shape, jnp.float32),
            pltpu.VMEM((TILE_PX, TILE_PX), jnp.bfloat16),
            pltpu.VMEM((ROWS, 128), jnp.float32),
            pltpu.VMEM((HALO, 128), jnp.bfloat16),
            pltpu.VMEM((TILE_PX, TILE_PX), jnp.float32),
            pltpu.VMEM((2, FREQ, FREQ), jnp.float32),
            pltpu.VMEM((SOURCES, GRID, 2 * GRID), jnp.float32),
            pltpu.VMEM((TILE_PX, 2 * GRID), jnp.bfloat16),
            pltpu.VMEM((2, FREQ, FREQ), jnp.float32),
            pltpu.SemaphoreType.DMA((13,)),
        ],
        compiler_params=pltpu.CompilerParams(vmem_limit_bytes=ALL_VMEM),
        interpret=INTERPRET,
        name="fields",
    )(slot_pos, ints, *arrays)


def steps_kernel(back_ref, col_ref, steps_hbm, edge_ref, steps_ref, sems):
    my_src = lax.axis_index("src")
    high, low = halves(-LEARN_RATE * back_ref[...])
    steps_ref[...] = dot_t(high, col_ref[...]) + dot_t(low, col_ref[...])
    keep = pltpu.make_async_copy(steps_ref, steps_hbm, sems.at[0])
    keep.start()
    at_end = my_src == SRC_DEVICES - 1
    edge_ref[...] = jnp.where(at_end, steps_ref[ROWS - HALO :, :], steps_ref[:HALO, :])
    keep.wait()


def make_steps(back, col):
    return pl.pallas_call(
        steps_kernel,
        out_shape=(
            jax.ShapeDtypeStruct((ROWS, TILE_PX), jnp.float32),
            jax.ShapeDtypeStruct((HALO, TILE_PX), jnp.float32),
        ),
        in_specs=[WHOLE, WHOLE],
        out_specs=[LEFT_THERE, WHOLE],
        scratch_shapes=[pltpu.VMEM((ROWS, TILE_PX), jnp.float32), pltpu.SemaphoreType.DMA((1,))],
        compiler_params=pltpu.CompilerParams(vmem_limit_bytes=4 * MIB),
        interpret=INTERPRET,
        name="steps",
    )(back, col)


def edge_kernel(slot_ref, got_ref, other_ref, edge_ref, col_ref, steps_in, steps_hbm, sum_ref, sems):
    my_slot, my_src, above, below = places(slot_ref)
    first = my_src == 0
    last = my_src == SRC_DEVICES - 1
    comes_from = jnp.where(first, above, below)

    @pl.when((first | last) & (comes_from >= 0))
    def _():
        place = comes_from // 2
        same_core = lax.rem(comes_from, 2) == lax.rem(my_slot, 2)
        rim = jnp.where(same_core, got_ref[place].astype(jnp.float32), other_ref[place].astype(jnp.float32))
        sum_ref[...] = edge_ref[...] - LEARN_RATE * dot_t(rim.astype(jnp.bfloat16), col_ref[...])
        start = pl.multiple_of(jnp.where(first, 0, ROWS - HALO), HALO)
        keep = pltpu.make_async_copy(sum_ref, steps_hbm.at[pl.ds(start, HALO)], sems.at[0])
        keep.start()
        keep.wait()


def add_edge(slot_pos, got, other, edge, col, steps):
    return pl.pallas_call(
        edge_kernel,
        out_shape=jax.ShapeDtypeStruct((ROWS, TILE_PX), jnp.float32),
        in_specs=[SCALARS] + [WHOLE] * 4 + [LEFT_THERE],
        out_specs=LEFT_THERE,
        scratch_shapes=[pltpu.VMEM((HALO, TILE_PX), jnp.float32), pltpu.SemaphoreType.DMA((1,))],
        input_output_aliases={5: 0},
        compiler_params=pltpu.CompilerParams(vmem_limit_bytes=4 * MIB),
        interpret=INTERPRET,
        name="edge",
    )(slot_pos, got, other, edge, col, steps)


def pupil_tables(pupil_phase):
    window = pupil_phase[32:96, 32:96]
    real = jnp.where(DISC, jnp.cos(window), 0.0) * SCALE
    imag = jnp.where(DISC, jnp.sin(window), 0.0) * SCALE
    return jnp.stack([jnp.concatenate([real, real], axis=1), jnp.concatenate([-imag, imag], axis=1)])


def own_moments(tile, col, row_table):
    half = jnp.dot(tile, col, preferred_element_type=jnp.float32)
    rows = row_table[HALO : HALO + TILE_PX]
    return lax.dot_general(
        rows, half, (((0,), (0,)), ((), ())), precision=lax.Precision.HIGHEST, preferred_element_type=jnp.float32
    )


def all_sources(src_shift, src_weight):
    swap = lambda value, mask: lax.ppermute(value, "src", [(i, i ^ mask) for i in range(SRC_DEVICES)])
    shifts = jnp.concatenate([src_shift, swap(src_shift, 4)], axis=0)
    weights = jnp.concatenate([src_weight, swap(src_weight, 4)], axis=0)
    ints = jnp.concatenate([shifts, weights[:, None]], axis=1)
    return jnp.concatenate([ints] + [swap(ints, mask) for mask in (1, 2, 3)], axis=0)


def per_device(mask_tiles, slot_pos, src_shift, src_weight, pupil_phase, target):
    ints = all_sources(src_shift, src_weight)
    col = jnp.asarray(COL)
    row_table = lax.optimization_barrier(jnp.asarray(ROW_F32))
    tile = mask_tiles[0]
    got = lax.all_to_all(make_rims(slot_pos, tile, col), "tile", 0, 0, tiled=True)
    own = own_moments(tile, col, row_table)
    small = jnp.asarray(SMALL)
    grids = jnp.asarray(GRIDS)
    flipped, right_t = flip_tables(small, grids)
    resist, back, sent = make_fields(
        slot_pos, ints, got, own, pupil_tables(pupil_phase), small, right_t, grids, flipped, row_table, target[0]
    )
    cores = [[2 * chip + core for chip in range(TILES // 2)] for core in range(2)]
    got = lax.all_to_all(sent, "tile", 0, 0, tiled=True, axis_index_groups=cores)
    steps, edge = make_steps(back, col)
    got, edge = lax.optimization_barrier((got, edge))
    other = lax.ppermute(got, "tile", [(i, i ^ 1) for i in range(TILES)])
    return (resist[None], add_edge(slot_pos, got, other, edge, col, steps)[None])


def solution(mesh):
    return jax.shard_map(
        per_device,
        mesh=mesh,
        in_specs=(P("tile", None, None), P(), P("src", None), P("src"), P(), P("tile", None, None)),
        out_specs=(P("tile", "src", None), P("tile", "src", None)),
        check_vma=False,
    )
```

```python
import math

import jax
import jax.numpy as jnp
import ml_dtypes
import numpy as np
from jax import lax
from jax.experimental import pallas as pl
from jax.experimental.pallas import tpu as pltpu
from jax.sharding import PartitionSpec as P

TILE_PX = 1024
HALO = 64
EXT_PX = 1152
FREQ = 128
GRID = 128
SOURCES = 16
TILES = 32
SRC_DEVICES = 8
PUPIL_R = 28
ROWS = 128
STEEPNESS = 4.0
THRESHOLD = 0.6
LEARN_RATE = 8.0
SCALE = 1.0 / (FREQ / 2 * math.sqrt(EXT_PX * TILE_PX))
INTERPRET = False
BF16 = ml_dtypes.bfloat16


def split(table):
    high = table.astype(BF16)
    return high, (table - high.astype(np.float64)).astype(BF16)


def half_table(count, period):
    angle = 2 * np.pi * ((np.arange(count)[:, None] * np.arange(64)[None]) % period) / period
    return np.concatenate([np.cos(angle), np.sin(angle)], axis=1)


def unfold_tables():
    even = np.zeros((FREQ, 64))
    odd = np.zeros((FREQ, 64))
    for row, freq in enumerate(range(-64, 64)):
        if freq > -64:
            even[row, abs(freq)] = 1
            odd[row, abs(freq)] = np.sign(freq)
    return even, odd


def coarse_table():
    angle = 2 * np.pi * ((np.arange(GRID)[:, None] * (np.arange(64) - 32)[None]) % GRID) / GRID
    return np.cos(angle), np.sin(angle)


def interpolation(positions):
    apart = positions[:, None] - np.arange(GRID)[None]
    return np.cos(2 * np.pi * apart[:, :, None] * np.arange(-63, 64) / GRID).sum(axis=-1) / GRID


COL = half_table(TILE_PX, TILE_PX).astype(BF16)
ROW = half_table(EXT_PX, EXT_PX)
EVEN, ODD = unfold_tables()
COS_W, SIN_W = coarse_table()
ROW_F32 = ROW.astype(np.float32)
ZERO = np.zeros((FREQ, 64))
UNFOLD = np.concatenate(
    [np.concatenate([EVEN, ZERO], axis=1), np.concatenate([ZERO, ODD], axis=1)], axis=0
)
LEFT_H, LEFT_L = split(np.concatenate([COS_W, SIN_W], axis=0))
RIGHT = np.concatenate(
    split(
        np.concatenate(
            [np.concatenate([COS_W.T, SIN_W.T], axis=1), np.concatenate([-SIN_W.T, COS_W.T], axis=1)], axis=0
        )
    ),
    axis=0,
)
LEFT_T = np.concatenate(split(np.concatenate([COS_W.T, SIN_W.T], axis=0)), axis=0)
RIM = np.concatenate(split(np.concatenate([ROW[:HALO], ROW[EXT_PX - HALO :]], axis=0).T), axis=1)
LANES = np.concatenate([EVEN, ODD], axis=1)
SMALL = np.concatenate(
    [
        UNFOLD.astype(BF16),
        np.concatenate([LEFT_H, LEFT_H, LEFT_L, np.zeros_like(LEFT_L)], axis=1),
        RIGHT,
        LEFT_T,
        np.concatenate([RIM, UNFOLD.T.astype(BF16)], axis=0),
        np.concatenate([LANES, np.zeros_like(LANES)], axis=0).astype(BF16),
    ],
    axis=1,
)
ROWS_Y = (HALO + np.arange(TILE_PX)) / 9.0
GRIDS = np.concatenate(split(interpolation(ROWS_Y)) + split(interpolation(np.arange(TILE_PX) / 8.0)), axis=1)
DISC = (np.arange(64)[:, None] - 32) ** 2 + (np.arange(64)[None] - 32) ** 2 <= PUPIL_R * PUPIL_R


def dot(left, right):
    return jnp.dot(left, right, preferred_element_type=jnp.float32)


def dot_t(left, right):
    return lax.dot_general(left, right, (((1,), (1,)), ((), ())), preferred_element_type=jnp.float32)


def halves(value):
    high = value.astype(jnp.bfloat16)
    return high, (value - high.astype(jnp.float32)).astype(jnp.bfloat16)


def low_lanes(shape):
    return lax.broadcasted_iota(jnp.int32, shape, 1) < 64


def places(slot_ref):
    my_slot = lax.axis_index("tile")
    my_position = slot_ref[my_slot]
    above = jnp.int32(-1)
    below = jnp.int32(-1)
    for slot in range(TILES):
        position = slot_ref[slot]
        above = jnp.where(position == my_position - 1, slot, above)
        below = jnp.where(position == my_position + 1, slot, below)
    return my_slot, lax.axis_index("src"), above, below


def rims_kernel(slot_ref, tile_hbm, col_hbm, sent_hbm, rows_ref, col_ref, rims_ref, sems):
    copies = [
        pltpu.make_async_copy(col_hbm, col_ref, sems.at[0]),
        pltpu.make_async_copy(tile_hbm.at[pl.ds(0, HALO)], rows_ref.at[pl.ds(0, HALO)], sems.at[1]),
        pltpu.make_async_copy(
            tile_hbm.at[pl.ds(TILE_PX - HALO, HALO)], rows_ref.at[pl.ds(HALO, HALO)], sems.at[2]
        ),
    ]
    for copy in copies:
        copy.start()
    my_slot, my_src, above, below = places(slot_ref)
    for copy in copies:
        copy.wait()
    rims_ref[...] = dot(rows_ref[...], col_ref[...]).astype(jnp.bfloat16).reshape(2, HALO, 128)

    for number, slot in enumerate((above, below)):

        @pl.when(slot >= 0)
        def _():
            pltpu.make_async_copy(rims_ref.at[number], sent_hbm.at[slot], sems.at[3 + number]).start()

    for number, slot in enumerate((above, below)):

        @pl.when(slot >= 0)
        def _():
            pltpu.make_async_copy(rims_ref.at[number], sent_hbm.at[slot], sems.at[3 + number]).wait()


SCALARS = pl.BlockSpec(memory_space=pltpu.SMEM)
WHOLE = pl.BlockSpec(memory_space=pltpu.VMEM)
LEFT_THERE = pl.BlockSpec(memory_space=pltpu.MemorySpace.HBM)
MIB = 1024 * 1024
ALL_VMEM = 63_000_000
FIELDS_VMEM = 54_000_000


def make_rims(slot_pos, tile, col):
    return pl.pallas_call(
        rims_kernel,
        out_shape=jax.ShapeDtypeStruct((TILES, HALO, 128), jnp.bfloat16),
        in_specs=[SCALARS, LEFT_THERE, LEFT_THERE],
        out_specs=LEFT_THERE,
        scratch_shapes=[
            pltpu.VMEM((2 * HALO, TILE_PX), jnp.bfloat16),
            pltpu.VMEM((TILE_PX, 128), jnp.bfloat16),
            pltpu.VMEM((2, HALO, 128), jnp.bfloat16),
            pltpu.SemaphoreType.DMA((5,)),
        ],
        compiler_params=pltpu.CompilerParams(vmem_limit_bytes=ALL_VMEM),
        interpret=INTERPRET,
        name="rims",
    )(slot_pos, tile, col)


def prep_kernel(small_hbm, grids_hbm, flipped_hbm, right_t_hbm, small_ref, grids_ref, flipped_ref, right_t_ref, sems):
    fetches = [
        pltpu.make_async_copy(grids_hbm, grids_ref, sems.at[0]),
        pltpu.make_async_copy(small_hbm.at[:, pl.ds(384, 256)], small_ref, sems.at[1]),
    ]
    keeps = [
        pltpu.make_async_copy(flipped_ref, flipped_hbm, sems.at[2]),
        pltpu.make_async_copy(right_t_ref, right_t_hbm, sems.at[3]),
    ]
    for fetch in fetches:
        fetch.start()
    fetches[0].wait()
    flipped_ref[...] = grids_ref[...].T
    keeps[0].start()
    fetches[1].wait()
    right_t_ref[...] = small_ref[...].T
    keeps[1].start()
    for keep in keeps:
        keep.wait()


def flip_tables(small, grids):
    return pl.pallas_call(
        prep_kernel,
        out_shape=(
            jax.ShapeDtypeStruct(GRIDS.shape[::-1], jnp.bfloat16),
            jax.ShapeDtypeStruct((256, 256), jnp.bfloat16),
        ),
        in_specs=[LEFT_THERE] * 2,
        out_specs=[LEFT_THERE] * 2,
        scratch_shapes=[
            pltpu.VMEM((256, 256), jnp.bfloat16),
            pltpu.VMEM(GRIDS.shape, jnp.bfloat16),
            pltpu.VMEM(GRIDS.shape[::-1], jnp.bfloat16),
            pltpu.VMEM((256, 256), jnp.bfloat16),
            pltpu.SemaphoreType.DMA((4,)),
        ],
        compiler_params=pltpu.CompilerParams(vmem_limit_bytes=ALL_VMEM),
        interpret=INTERPRET,
        name="prep",
    )(small, grids)


def fields_kernel(
    slot_ref, ints_ref, got_ref, own_ref, pupil_ref, small_ref, right_t_ref, row_ref, grids_hbm, flipped_hbm, target_hbm,
    resist_hbm, back_ref, sent_hbm,
    edge_ref, grids_ref, flipped_ref, target_ref, resist_ref, spec_ref, field_ref, fold_ref, grad_ref, sems,
):
    fetches = [
        pltpu.make_async_copy(source, target, sems.at[number])
        for number, (source, target) in enumerate(
            ((grids_hbm, grids_ref), (flipped_hbm, flipped_ref), (target_hbm, target_ref))
        )
    ]
    for fetch in fetches:
        fetch.start()
    my_slot, my_src, above, below = places(slot_ref)
    unfold = small_ref[:, 0:128]
    left = small_ref[:, 128:320]
    right = small_ref[:, 384:640]
    left_t = small_ref[:, 640:768]
    rim_table = small_ref[:128, 768:1024]
    unfold_t = small_ref[128:, 768:1024]
    lanes = small_ref[:128, 1024:1152]
    lanes2 = jnp.concatenate([lanes, lanes], axis=1)
    low = low_lanes((128, 128))
    low_w = low_lanes((64, 128))
    up = jnp.where(above >= 0, got_ref[jnp.maximum(above, 0)].astype(jnp.float32), 0.0)
    down = jnp.where(below >= 0, got_ref[jnp.maximum(below, 0)].astype(jnp.float32), 0.0)
    rims = jnp.concatenate([up, down], axis=0).astype(jnp.bfloat16)
    moments = own_ref[...] + dot(rim_table, jnp.concatenate([rims, rims], axis=0))
    half = dot(jnp.concatenate([unfold, unfold], axis=1), jnp.concatenate(halves(moments), axis=0))
    by_cos, by_sin = half[:FREQ], half[FREQ:]
    spec_ref[0] = dot_t(jnp.concatenate(halves(jnp.where(low, by_cos, -by_sin)), axis=1), lanes2)
    spec_ref[1] = dot_t(jnp.concatenate(halves(jnp.where(low, -by_sin, -by_cos)), axis=1), lanes2)
    coarse = jnp.zeros((GRID, GRID), jnp.float32)
    for source in range(SOURCES):
        shift_a = ints_ref[source, 0]
        shift_b = ints_ref[source, 1]
        rows = pl.ds(32 - shift_a, 64)
        spec_re = spec_ref[0, rows, :]
        spec_im = spec_ref[1, rows, :]
        near = lax.rem(96 + shift_b, 128)
        far = 32 + shift_b
        window = jnp.where(low_w, pltpu.roll(spec_re, near, 1), pltpu.roll(spec_im, far, 1))
        amp = pupil_ref[0] * window + pupil_ref[1] * pltpu.roll(window, 64, 1)
        amp_h, amp_l = halves(amp)
        both = dot(left, jnp.concatenate([amp_h, amp_l, amp_h], axis=0))
        swapped = pltpu.roll(both[GRID:], 64, 1)
        line = both[:GRID] + jnp.where(low, -swapped, swapped)
        line_h, line_l = halves(line)
        field = dot(jnp.concatenate([line_h, line_h], axis=1), right) + dot(line_l, right[:128])
        field_ref[source] = field
        weight = ints_ref[source, 2].astype(jnp.float32) * (1.0 / (4.0 * SOURCES))
        squared = field * field
        coarse = coarse + weight * (squared[:, :GRID] + squared[:, GRID:])
    coarse_h, coarse_l = halves(coarse)
    coarse_hh = jnp.concatenate([coarse_h, coarse_h], axis=0)
    for fetch in fetches:
        fetch.wait()
    grid_x = grids_ref[:, 256:512]
    grid_xhh = jnp.concatenate([flipped_ref[256:384, :], flipped_ref[256:384, :]], axis=0)
    grid_yt = flipped_ref[0:256, :]
    chunk = 256
    for place in range(TILE_PX // chunk):
        rows = pl.ds(place * chunk, chunk)
        rows_y = dot(grids_ref[rows, 0:256], coarse_hh) + dot(grids_ref[rows, 0:128], coarse_l)
        rows_h, rows_l = halves(rows_y)
        intensity = dot(jnp.concatenate([rows_h, rows_l], axis=1), grid_xhh)
        resist = jax.nn.sigmoid(STEEPNESS * (intensity - THRESHOLD))
        resist_ref[rows, :] = resist
        wanted = target_ref[rows, :].astype(jnp.float32)
        adjoint = ((2.0 * STEEPNESS) * (resist - wanted) * resist * (1.0 - resist)).astype(jnp.bfloat16)
        folded = dot(adjoint, grid_x)
        fold_ref[rows, :] = jnp.concatenate(halves(folded[:, :GRID] + folded[:, GRID:]), axis=1)
    mine = pl.multiple_of(my_src * ROWS, ROWS)
    keep = pltpu.make_async_copy(resist_ref.at[pl.ds(mine, ROWS)], resist_hbm, sems.at[3])
    keep.start()
    adjoint4 = dot(grid_yt, fold_ref[...])
    adjoint2 = adjoint4[:GRID] + adjoint4[GRID:]
    coarse_adjoint = 2.0 * (adjoint2[:, :GRID] + adjoint2[:, GRID:])
    right_t = right_t_ref[...]
    grad_ref[...] = jnp.zeros(grad_ref.shape, jnp.float32)
    for source in range(SOURCES):
        shift_a = ints_ref[source, 0]
        shift_b = ints_ref[source, 1]
        weight = ints_ref[source, 2].astype(jnp.float32) * (1.0 / (4.0 * SOURCES))
        weighted = weight * coarse_adjoint
        dfield_h, dfield_l = halves(field_ref[source] * jnp.concatenate([weighted, weighted], axis=1))
        dline2 = dot(dfield_h, right_t)
        dline = dline2[:, :128] + dline2[:, 128:] + dot(dfield_l, right_t[:, :128])
        damp4 = dot(left_t, jnp.concatenate(halves(dline), axis=1))
        damp2 = damp4[:128] + damp4[128:]
        damp1 = damp2[:, :128] + damp2[:, 128:]
        swapped = pltpu.roll(damp1[64:], 64, 1)
        damp = damp1[:64] + jnp.where(low_w, swapped, -swapped)
        grad = pupil_ref[0] * damp - pupil_ref[1] * pltpu.roll(damp, 64, 1)
        rows = pl.ds(32 - shift_a, 64)
        grad_ref[0, rows, :] += pltpu.roll(jnp.where(low_w, grad, 0.0), 32 - shift_b, 1)
        grad_ref[1, rows, :] += pltpu.roll(jnp.where(low_w, 0.0, grad), lax.rem(96 - shift_b, 128), 1)
    grads = jnp.concatenate([grad_ref[0], grad_ref[1]], axis=0)
    folded = dot(jnp.concatenate(halves(grads), axis=1), jnp.concatenate([lanes, lanes], axis=0))
    fold_re, fold_im = folded[:FREQ], folded[FREQ:]
    packed = jnp.concatenate(
        [jnp.where(low, fold_re, -fold_im), jnp.where(low, -fold_im, -fold_re)], axis=0
    )
    packed = dot(jnp.concatenate([unfold_t, unfold_t], axis=1), jnp.concatenate(halves(packed), axis=0))
    first = my_src == 0
    edge_rows = row_ref[pl.ds(pl.multiple_of(jnp.where(first, EXT_PX - HALO, 0), HALO), HALO), :]
    mine_rows = row_ref[pl.ds(pl.multiple_of(HALO + my_src * ROWS, HALO), ROWS), :]
    tables = jnp.concatenate([edge_rows, mine_rows], axis=0)
    back = jnp.dot(tables, packed, precision=lax.Precision.HIGHEST, preferred_element_type=jnp.float32)
    goes_to = jnp.where(first, below, above)

    @pl.when(goes_to >= 0)
    def _():
        edge_ref[...] = back[:HALO].astype(jnp.bfloat16)
        send = pltpu.make_async_copy(edge_ref, sent_hbm.at[goes_to // 2], sems.at[4])
        send.start()
        send.wait()

    back_ref[...] = back[HALO:]
    keep.wait()


def make_fields(slot_pos, ints, *arrays):
    return pl.pallas_call(
        fields_kernel,
        out_shape=(
            jax.ShapeDtypeStruct((ROWS, TILE_PX), jnp.float32),
            jax.ShapeDtypeStruct((ROWS, 128), jnp.float32),
            jax.ShapeDtypeStruct((TILES // 2, HALO, 128), jnp.bfloat16),
        ),
        in_specs=[SCALARS, SCALARS] + [WHOLE] * 6 + [LEFT_THERE] * 3,
        out_specs=[LEFT_THERE, WHOLE, LEFT_THERE],
        scratch_shapes=[
            pltpu.VMEM((HALO, 128), jnp.bfloat16),
            pltpu.VMEM(GRIDS.shape, jnp.bfloat16),
            pltpu.VMEM(GRIDS.shape[::-1], jnp.bfloat16),
            pltpu.VMEM((TILE_PX, TILE_PX), jnp.bfloat16),
            pltpu.VMEM((TILE_PX, TILE_PX), jnp.float32),
            pltpu.VMEM((2, FREQ, FREQ), jnp.float32),
            pltpu.VMEM((SOURCES, GRID, 2 * GRID), jnp.float32),
            pltpu.VMEM((TILE_PX, 2 * GRID), jnp.bfloat16),
            pltpu.VMEM((2, FREQ, FREQ), jnp.float32),
            pltpu.SemaphoreType.DMA((5,)),
        ],
        compiler_params=pltpu.CompilerParams(vmem_limit_bytes=FIELDS_VMEM),
        interpret=INTERPRET,
        name="fields",
    )(slot_pos, ints, *arrays)


def steps_kernel(back_ref, col_ref, steps_hbm, edge_ref, steps_ref, sems):
    my_src = lax.axis_index("src")
    high, low = halves(-LEARN_RATE * back_ref[...])
    steps_ref[...] = dot_t(high, col_ref[...]) + dot_t(low, col_ref[...])
    keep = pltpu.make_async_copy(steps_ref, steps_hbm, sems.at[0])
    keep.start()
    at_end = my_src == SRC_DEVICES - 1
    edge_ref[...] = jnp.where(at_end, steps_ref[ROWS - HALO :, :], steps_ref[:HALO, :])
    keep.wait()


def make_steps(back, col):
    return pl.pallas_call(
        steps_kernel,
        out_shape=(
            jax.ShapeDtypeStruct((ROWS, TILE_PX), jnp.float32),
            jax.ShapeDtypeStruct((HALO, TILE_PX), jnp.float32),
        ),
        in_specs=[WHOLE, WHOLE],
        out_specs=[LEFT_THERE, WHOLE],
        scratch_shapes=[pltpu.VMEM((ROWS, TILE_PX), jnp.float32), pltpu.SemaphoreType.DMA((1,))],
        compiler_params=pltpu.CompilerParams(vmem_limit_bytes=4 * MIB),
        interpret=INTERPRET,
        name="steps",
    )(back, col)


def edge_kernel(slot_ref, got_ref, other_ref, edge_ref, col_ref, steps_in, steps_hbm, sum_ref, sems):
    my_slot, my_src, above, below = places(slot_ref)
    first = my_src == 0
    last = my_src == SRC_DEVICES - 1
    comes_from = jnp.where(first, above, below)

    @pl.when((first | last) & (comes_from >= 0))
    def _():
        place = comes_from // 2
        same_core = lax.rem(comes_from, 2) == lax.rem(my_slot, 2)
        rim = jnp.where(same_core, got_ref[place].astype(jnp.float32), other_ref[place].astype(jnp.float32))
        sum_ref[...] = edge_ref[...] - LEARN_RATE * dot_t(rim.astype(jnp.bfloat16), col_ref[...])
        start = pl.multiple_of(jnp.where(first, 0, ROWS - HALO), HALO)
        keep = pltpu.make_async_copy(sum_ref, steps_hbm.at[pl.ds(start, HALO)], sems.at[0])
        keep.start()
        keep.wait()


def add_edge(slot_pos, got, other, edge, col, steps):
    return pl.pallas_call(
        edge_kernel,
        out_shape=jax.ShapeDtypeStruct((ROWS, TILE_PX), jnp.float32),
        in_specs=[SCALARS] + [WHOLE] * 4 + [LEFT_THERE],
        out_specs=LEFT_THERE,
        scratch_shapes=[pltpu.VMEM((HALO, TILE_PX), jnp.float32), pltpu.SemaphoreType.DMA((1,))],
        input_output_aliases={5: 0},
        compiler_params=pltpu.CompilerParams(vmem_limit_bytes=4 * MIB),
        interpret=INTERPRET,
        name="edge",
    )(slot_pos, got, other, edge, col, steps)


def pupil_tables(pupil_phase):
    window = pupil_phase[32:96, 32:96]
    real = jnp.where(DISC, jnp.cos(window), 0.0) * SCALE
    imag = jnp.where(DISC, jnp.sin(window), 0.0) * SCALE
    return jnp.stack([jnp.concatenate([real, real], axis=1), jnp.concatenate([-imag, imag], axis=1)])


def own_moments(tile, col, row_table):
    half = jnp.dot(tile, col, preferred_element_type=jnp.float32)
    rows = row_table[HALO : HALO + TILE_PX]
    return lax.dot_general(
        rows, half, (((0,), (0,)), ((), ())), precision=lax.Precision.HIGHEST, preferred_element_type=jnp.float32
    )


def all_sources(src_shift, src_weight):
    swap = lambda value, mask: lax.ppermute(value, "src", [(i, i ^ mask) for i in range(SRC_DEVICES)])
    shifts = jnp.concatenate([src_shift, swap(src_shift, 4)], axis=0)
    weights = jnp.concatenate([src_weight, swap(src_weight, 4)], axis=0)
    ints = jnp.concatenate([shifts, weights[:, None]], axis=1)
    return jnp.concatenate([ints] + [swap(ints, mask) for mask in (1, 2, 3)], axis=0)


def per_device(mask_tiles, slot_pos, src_shift, src_weight, pupil_phase, target):
    ints = all_sources(src_shift, src_weight)
    col = jnp.asarray(COL)
    row_table = lax.optimization_barrier(jnp.asarray(ROW_F32))
    tile = mask_tiles[0]
    got = lax.all_to_all(make_rims(slot_pos, tile, col), "tile", 0, 0, tiled=True)
    own = own_moments(tile, col, row_table)
    small = jnp.asarray(SMALL)
    grids = jnp.asarray(GRIDS)
    flipped, right_t = flip_tables(small, grids)
    resist, back, sent = make_fields(
        slot_pos, ints, got, own, pupil_tables(pupil_phase), small, right_t, row_table, grids, flipped, target[0]
    )
    cores = [[2 * chip + core for chip in range(TILES // 2)] for core in range(2)]
    got = lax.all_to_all(sent, "tile", 0, 0, tiled=True, axis_index_groups=cores)
    steps, edge = make_steps(back, col)
    got, edge = lax.optimization_barrier((got, edge))
    other = lax.ppermute(got, "tile", [(i, i ^ 1) for i in range(TILES)])
    return (resist[None], add_edge(slot_pos, got, other, edge, col, steps)[None])


def solution(mesh):
    return jax.shard_map(
        per_device,
        mesh=mesh,
        in_specs=(P("tile", None, None), P(), P("src", None), P("src"), P(), P("tile", None, None)),
        out_specs=(P("tile", "src", None), P("tile", "src", None)),
        check_vma=False,
    )
```

```python
import math

import jax
import jax.numpy as jnp
import ml_dtypes
import numpy as np
from jax import lax
from jax.experimental import pallas as pl
from jax.experimental.pallas import tpu as pltpu
from jax.sharding import PartitionSpec as P

TILE_PX = 1024
HALO = 64
EXT_PX = 1152
FREQ = 128
GRID = 128
SOURCES = 16
TILES = 32
SRC_DEVICES = 8
PUPIL_R = 28
ROWS = 128
STEEPNESS = 4.0
THRESHOLD = 0.6
LEARN_RATE = 8.0
SCALE = 1.0 / (FREQ / 2 * math.sqrt(EXT_PX * TILE_PX))
INTERPRET = False
BF16 = ml_dtypes.bfloat16


def split(table):
    high = table.astype(BF16)
    return high, (table - high.astype(np.float64)).astype(BF16)


def half_table(count, period):
    angle = 2 * np.pi * ((np.arange(count)[:, None] * np.arange(64)[None]) % period) / period
    return np.concatenate([np.cos(angle), np.sin(angle)], axis=1)


def unfold_tables():
    even = np.zeros((FREQ, 64))
    odd = np.zeros((FREQ, 64))
    for row, freq in enumerate(range(-64, 64)):
        if freq > -64:
            even[row, abs(freq)] = 1
            odd[row, abs(freq)] = np.sign(freq)
    return even, odd


def coarse_table():
    angle = 2 * np.pi * ((np.arange(GRID)[:, None] * (np.arange(64) - 32)[None]) % GRID) / GRID
    return np.cos(angle), np.sin(angle)


def interpolation(positions):
    apart = positions[:, None] - np.arange(GRID)[None]
    return np.cos(2 * np.pi * apart[:, :, None] * np.arange(-63, 64) / GRID).sum(axis=-1) / GRID


COL = half_table(TILE_PX, TILE_PX).astype(BF16)
ROW = half_table(EXT_PX, EXT_PX)
EVEN, ODD = unfold_tables()
COS_W, SIN_W = coarse_table()
ROW_F32 = ROW.astype(np.float32)
ZERO = np.zeros((FREQ, 64))
UNFOLD = np.concatenate(
    [np.concatenate([EVEN, ZERO], axis=1), np.concatenate([ZERO, ODD], axis=1)], axis=0
)
LEFT_H, LEFT_L = split(np.concatenate([COS_W, SIN_W], axis=0))
RIGHT = np.concatenate(
    split(
        np.concatenate(
            [np.concatenate([COS_W.T, SIN_W.T], axis=1), np.concatenate([-SIN_W.T, COS_W.T], axis=1)], axis=0
        )
    ),
    axis=0,
)
LEFT_T = np.concatenate(split(np.concatenate([COS_W.T, SIN_W.T], axis=0)), axis=0)
RIM = np.concatenate(split(np.concatenate([ROW[:HALO], ROW[EXT_PX - HALO :]], axis=0).T), axis=1)
LANES = np.concatenate([EVEN, ODD], axis=1)
SMALL = np.concatenate(
    [
        UNFOLD.astype(BF16),
        np.concatenate([LEFT_H, LEFT_H, LEFT_L, np.zeros_like(LEFT_L)], axis=1),
        RIGHT,
        LEFT_T,
        np.concatenate([RIM, UNFOLD.T.astype(BF16)], axis=0),
        np.concatenate([LANES, np.zeros_like(LANES)], axis=0).astype(BF16),
    ],
    axis=1,
)
ROWS_Y = (HALO + np.arange(TILE_PX)) / 9.0
GRIDS = np.concatenate(split(interpolation(ROWS_Y)) + split(interpolation(np.arange(TILE_PX) / 8.0)), axis=1)
DISC = (np.arange(64)[:, None] - 32) ** 2 + (np.arange(64)[None] - 32) ** 2 <= PUPIL_R * PUPIL_R


def dot(left, right):
    return jnp.dot(left, right, preferred_element_type=jnp.float32)


def dot_t(left, right):
    return lax.dot_general(left, right, (((1,), (1,)), ((), ())), preferred_element_type=jnp.float32)


def halves(value):
    high = value.astype(jnp.bfloat16)
    return high, (value - high.astype(jnp.float32)).astype(jnp.bfloat16)


def low_lanes(shape):
    return lax.broadcasted_iota(jnp.int32, shape, 1) < 64


def places(slot_ref):
    my_slot = lax.axis_index("tile")
    my_position = slot_ref[my_slot]
    above = jnp.int32(-1)
    below = jnp.int32(-1)
    for slot in range(TILES):
        position = slot_ref[slot]
        above = jnp.where(position == my_position - 1, slot, above)
        below = jnp.where(position == my_position + 1, slot, below)
    return my_slot, lax.axis_index("src"), above, below


def rims_kernel(slot_ref, tile_hbm, col_hbm, sent_hbm, rows_ref, col_ref, rims_ref, sems):
    copies = [
        pltpu.make_async_copy(col_hbm, col_ref, sems.at[0]),
        pltpu.make_async_copy(tile_hbm.at[pl.ds(0, HALO)], rows_ref.at[pl.ds(0, HALO)], sems.at[1]),
        pltpu.make_async_copy(
            tile_hbm.at[pl.ds(TILE_PX - HALO, HALO)], rows_ref.at[pl.ds(HALO, HALO)], sems.at[2]
        ),
    ]
    for copy in copies:
        copy.start()
    my_slot, my_src, above, below = places(slot_ref)
    for copy in copies:
        copy.wait()
    rims_ref[...] = dot(rows_ref[...], col_ref[...]).astype(jnp.bfloat16).reshape(2, HALO, 128)

    for number, slot in enumerate((above, below)):

        @pl.when(slot >= 0)
        def _():
            pltpu.make_async_copy(rims_ref.at[number], sent_hbm.at[slot], sems.at[3 + number]).start()

    for number, slot in enumerate((above, below)):

        @pl.when(slot >= 0)
        def _():
            pltpu.make_async_copy(rims_ref.at[number], sent_hbm.at[slot], sems.at[3 + number]).wait()


SCALARS = pl.BlockSpec(memory_space=pltpu.SMEM)
WHOLE = pl.BlockSpec(memory_space=pltpu.VMEM)
LEFT_THERE = pl.BlockSpec(memory_space=pltpu.MemorySpace.HBM)
MIB = 1024 * 1024
ALL_VMEM = 63_000_000
FIELDS_VMEM = 54_000_000


def make_rims(slot_pos, tile, col):
    return pl.pallas_call(
        rims_kernel,
        out_shape=jax.ShapeDtypeStruct((TILES, HALO, 128), jnp.bfloat16),
        in_specs=[SCALARS, LEFT_THERE, LEFT_THERE],
        out_specs=LEFT_THERE,
        scratch_shapes=[
            pltpu.VMEM((2 * HALO, TILE_PX), jnp.bfloat16),
            pltpu.VMEM((TILE_PX, 128), jnp.bfloat16),
            pltpu.VMEM((2, HALO, 128), jnp.bfloat16),
            pltpu.SemaphoreType.DMA((5,)),
        ],
        compiler_params=pltpu.CompilerParams(vmem_limit_bytes=ALL_VMEM),
        interpret=INTERPRET,
        name="rims",
    )(slot_pos, tile, col)


def prep_kernel(small_hbm, grids_hbm, flipped_hbm, right_t_hbm, small_ref, grids_ref, flipped_ref, right_t_ref, sems):
    fetches = [
        pltpu.make_async_copy(grids_hbm, grids_ref, sems.at[0]),
        pltpu.make_async_copy(small_hbm.at[:, pl.ds(384, 256)], small_ref, sems.at[1]),
    ]
    keeps = [
        pltpu.make_async_copy(flipped_ref, flipped_hbm, sems.at[2]),
        pltpu.make_async_copy(right_t_ref, right_t_hbm, sems.at[3]),
    ]
    for fetch in fetches:
        fetch.start()
    fetches[0].wait()
    flipped_ref[...] = grids_ref[...].T
    keeps[0].start()
    fetches[1].wait()
    right_t_ref[...] = small_ref[...].T
    keeps[1].start()
    for keep in keeps:
        keep.wait()


def flip_tables(small, grids):
    return pl.pallas_call(
        prep_kernel,
        out_shape=(
            jax.ShapeDtypeStruct(GRIDS.shape[::-1], jnp.bfloat16),
            jax.ShapeDtypeStruct((256, 256), jnp.bfloat16),
        ),
        in_specs=[LEFT_THERE] * 2,
        out_specs=[LEFT_THERE] * 2,
        scratch_shapes=[
            pltpu.VMEM((256, 256), jnp.bfloat16),
            pltpu.VMEM(GRIDS.shape, jnp.bfloat16),
            pltpu.VMEM(GRIDS.shape[::-1], jnp.bfloat16),
            pltpu.VMEM((256, 256), jnp.bfloat16),
            pltpu.SemaphoreType.DMA((4,)),
        ],
        compiler_params=pltpu.CompilerParams(vmem_limit_bytes=ALL_VMEM),
        interpret=INTERPRET,
        name="prep",
    )(small, grids)


def fields_kernel(
    slot_ref, ints_ref, got_ref, own_ref, pupil_ref, small_ref, right_t_ref, row_ref, grids_hbm, flipped_hbm, target_hbm,
    resist_hbm, back_ref, sent_hbm,
    edge_ref, grids_ref, flipped_ref, target_ref, resist_ref, spec_ref, field_ref, fold_ref, grad_ref, sems,
):
    fetches = [
        pltpu.make_async_copy(source, target, sems.at[number])
        for number, (source, target) in enumerate(
            [(grids_hbm.at[:, pl.ds(0, 256)], grids_ref.at[:, pl.ds(0, 256)]), (flipped_hbm.at[pl.ds(256, 128)], flipped_ref.at[pl.ds(256, 128)])]
            + [(target_hbm.at[pl.ds(256 * part, 256)], target_ref.at[pl.ds(256 * part, 256)]) for part in range(4)]
            + [(grids_hbm.at[:, pl.ds(256, 256)], grids_ref.at[:, pl.ds(256, 256)]), (flipped_hbm.at[pl.ds(0, 256)], flipped_ref.at[pl.ds(0, 256)])]
        )
    ]
    fetches = [fetches[number] for number in (0, 1, 6, 2, 3, 4, 5, 7)]
    for fetch in fetches:
        fetch.start()
    my_slot, my_src, above, below = places(slot_ref)
    unfold = small_ref[:, 0:128]
    left = small_ref[:, 128:320]
    right = small_ref[:, 384:640]
    left_t = small_ref[:, 640:768]
    rim_table = small_ref[:128, 768:1024]
    unfold_t = small_ref[128:, 768:1024]
    lanes = small_ref[:128, 1024:1152]
    lanes2 = jnp.concatenate([lanes, lanes], axis=1)
    low = low_lanes((128, 128))
    low_w = low_lanes((64, 128))
    up = jnp.where(above >= 0, got_ref[jnp.maximum(above, 0)].astype(jnp.float32), 0.0)
    down = jnp.where(below >= 0, got_ref[jnp.maximum(below, 0)].astype(jnp.float32), 0.0)
    rims = jnp.concatenate([up, down], axis=0).astype(jnp.bfloat16)
    moments = own_ref[...] + dot(rim_table, jnp.concatenate([rims, rims], axis=0))
    half = dot(jnp.concatenate([unfold, unfold], axis=1), jnp.concatenate(halves(moments), axis=0))
    by_cos, by_sin = half[:FREQ], half[FREQ:]
    spec_ref[0] = dot_t(jnp.concatenate(halves(jnp.where(low, by_cos, -by_sin)), axis=1), lanes2)
    spec_ref[1] = dot_t(jnp.concatenate(halves(jnp.where(low, -by_sin, -by_cos)), axis=1), lanes2)
    coarse = jnp.zeros((GRID, GRID), jnp.float32)
    for source in range(SOURCES):
        shift_a = ints_ref[source, 0]
        shift_b = ints_ref[source, 1]
        rows = pl.ds(32 - shift_a, 64)
        spec_re = spec_ref[0, rows, :]
        spec_im = spec_ref[1, rows, :]
        near = lax.rem(96 + shift_b, 128)
        far = 32 + shift_b
        window = jnp.where(low_w, pltpu.roll(spec_re, near, 1), pltpu.roll(spec_im, far, 1))
        amp = pupil_ref[0] * window + pupil_ref[1] * pltpu.roll(window, 64, 1)
        amp_h, amp_l = halves(amp)
        both = dot(left, jnp.concatenate([amp_h, amp_l, amp_h], axis=0))
        swapped = pltpu.roll(both[GRID:], 64, 1)
        line = both[:GRID] + jnp.where(low, -swapped, swapped)
        line_h, line_l = halves(line)
        field = dot(jnp.concatenate([line_h, line_h], axis=1), right) + dot(line_l, right[:128])
        field_ref[source] = field
        weight = ints_ref[source, 2].astype(jnp.float32) * (1.0 / (4.0 * SOURCES))
        squared = field * field
        coarse = coarse + weight * (squared[:, :GRID] + squared[:, GRID:])
    coarse_h, coarse_l = halves(coarse)
    coarse_hh = jnp.concatenate([coarse_h, coarse_h], axis=0)
    for fetch in fetches[:3]:
        fetch.wait()
    grid_x = grids_ref[:, 256:512]
    grid_xhh = jnp.concatenate([flipped_ref[256:384, :], flipped_ref[256:384, :]], axis=0)
    chunk = 256
    for place in range(TILE_PX // chunk):
        rows = pl.ds(place * chunk, chunk)
        rows_y = dot(grids_ref[rows, 0:256], coarse_hh) + dot(grids_ref[rows, 0:128], coarse_l)
        rows_h, rows_l = halves(rows_y)
        intensity = dot(jnp.concatenate([rows_h, rows_l], axis=1), grid_xhh)
        resist = jax.nn.sigmoid(STEEPNESS * (intensity - THRESHOLD))
        resist_ref[rows, :] = resist
        fetches[3 + place].wait()
        wanted = target_ref[rows, :].astype(jnp.float32)
        adjoint = ((2.0 * STEEPNESS) * (resist - wanted) * resist * (1.0 - resist)).astype(jnp.bfloat16)
        folded = dot(adjoint, grid_x)
        fold_ref[rows, :] = jnp.concatenate(halves(folded[:, :GRID] + folded[:, GRID:]), axis=1)
    mine = pl.multiple_of(my_src * ROWS, ROWS)
    keep = pltpu.make_async_copy(resist_ref.at[pl.ds(mine, ROWS)], resist_hbm, sems.at[8])
    keep.start()
    fetches[7].wait()
    adjoint4 = dot(flipped_ref[0:256, :], fold_ref[...])
    adjoint2 = adjoint4[:GRID] + adjoint4[GRID:]
    coarse_adjoint = 2.0 * (adjoint2[:, :GRID] + adjoint2[:, GRID:])
    right_t = right_t_ref[...]
    grad_ref[...] = jnp.zeros(grad_ref.shape, jnp.float32)
    for source in range(SOURCES):
        shift_a = ints_ref[source, 0]
        shift_b = ints_ref[source, 1]
        weight = ints_ref[source, 2].astype(jnp.float32) * (1.0 / (4.0 * SOURCES))
        weighted = weight * coarse_adjoint
        dfield_h, dfield_l = halves(field_ref[source] * jnp.concatenate([weighted, weighted], axis=1))
        dline2 = dot(dfield_h, right_t)
        dline = dline2[:, :128] + dline2[:, 128:] + dot(dfield_l, right_t[:, :128])
        damp4 = dot(left_t, jnp.concatenate(halves(dline), axis=1))
        damp2 = damp4[:128] + damp4[128:]
        damp1 = damp2[:, :128] + damp2[:, 128:]
        swapped = pltpu.roll(damp1[64:], 64, 1)
        damp = damp1[:64] + jnp.where(low_w, swapped, -swapped)
        grad = pupil_ref[0] * damp - pupil_ref[1] * pltpu.roll(damp, 64, 1)
        rows = pl.ds(32 - shift_a, 64)
        grad_ref[0, rows, :] += pltpu.roll(jnp.where(low_w, grad, 0.0), 32 - shift_b, 1)
        grad_ref[1, rows, :] += pltpu.roll(jnp.where(low_w, 0.0, grad), lax.rem(96 - shift_b, 128), 1)
    grads = jnp.concatenate([grad_ref[0], grad_ref[1]], axis=0)
    folded = dot(jnp.concatenate(halves(grads), axis=1), jnp.concatenate([lanes, lanes], axis=0))
    fold_re, fold_im = folded[:FREQ], folded[FREQ:]
    packed = jnp.concatenate(
        [jnp.where(low, fold_re, -fold_im), jnp.where(low, -fold_im, -fold_re)], axis=0
    )
    packed = dot(jnp.concatenate([unfold_t, unfold_t], axis=1), jnp.concatenate(halves(packed), axis=0))
    first = my_src == 0
    edge_rows = row_ref[pl.ds(pl.multiple_of(jnp.where(first, EXT_PX - HALO, 0), HALO), HALO), :]
    mine_rows = row_ref[pl.ds(pl.multiple_of(HALO + my_src * ROWS, HALO), ROWS), :]
    tables = jnp.concatenate([edge_rows, mine_rows], axis=0)
    back = jnp.dot(tables, packed, precision=lax.Precision.HIGHEST, preferred_element_type=jnp.float32)
    goes_to = jnp.where(first, below, above)

    @pl.when(goes_to >= 0)
    def _():
        edge_ref[...] = back[:HALO].astype(jnp.bfloat16)
        send = pltpu.make_async_copy(edge_ref, sent_hbm.at[goes_to // 2], sems.at[9])
        send.start()
        send.wait()

    back_ref[...] = back[HALO:]
    keep.wait()


def make_fields(slot_pos, ints, *arrays):
    return pl.pallas_call(
        fields_kernel,
        out_shape=(
            jax.ShapeDtypeStruct((ROWS, TILE_PX), jnp.float32),
            jax.ShapeDtypeStruct((ROWS, 128), jnp.float32),
            jax.ShapeDtypeStruct((TILES // 2, HALO, 128), jnp.bfloat16),
        ),
        in_specs=[SCALARS, SCALARS] + [WHOLE] * 6 + [LEFT_THERE] * 3,
        out_specs=[LEFT_THERE, WHOLE, LEFT_THERE],
        scratch_shapes=[
            pltpu.VMEM((HALO, 128), jnp.bfloat16),
            pltpu.VMEM(GRIDS.shape, jnp.bfloat16),
            pltpu.VMEM(GRIDS.shape[::-1], jnp.bfloat16),
            pltpu.VMEM((TILE_PX, TILE_PX), jnp.bfloat16),
            pltpu.VMEM((TILE_PX, TILE_PX), jnp.float32),
            pltpu.VMEM((2, FREQ, FREQ), jnp.float32),
            pltpu.VMEM((SOURCES, GRID, 2 * GRID), jnp.float32),
            pltpu.VMEM((TILE_PX, 2 * GRID), jnp.bfloat16),
            pltpu.VMEM((2, FREQ, FREQ), jnp.float32),
            pltpu.SemaphoreType.DMA((10,)),
        ],
        compiler_params=pltpu.CompilerParams(vmem_limit_bytes=FIELDS_VMEM),
        interpret=INTERPRET,
        name="fields",
    )(slot_pos, ints, *arrays)


def steps_kernel(back_ref, col_ref, steps_hbm, edge_ref, steps_ref, sems):
    my_src = lax.axis_index("src")
    high, low = halves(-LEARN_RATE * back_ref[...])
    steps_ref[...] = dot_t(high, col_ref[...]) + dot_t(low, col_ref[...])
    keep = pltpu.make_async_copy(steps_ref, steps_hbm, sems.at[0])
    keep.start()
    at_end = my_src == SRC_DEVICES - 1
    edge_ref[...] = jnp.where(at_end, steps_ref[ROWS - HALO :, :], steps_ref[:HALO, :])
    keep.wait()


def make_steps(back, col):
    return pl.pallas_call(
        steps_kernel,
        out_shape=(
            jax.ShapeDtypeStruct((ROWS, TILE_PX), jnp.float32),
            jax.ShapeDtypeStruct((HALO, TILE_PX), jnp.float32),
        ),
        in_specs=[WHOLE, WHOLE],
        out_specs=[LEFT_THERE, WHOLE],
        scratch_shapes=[pltpu.VMEM((ROWS, TILE_PX), jnp.float32), pltpu.SemaphoreType.DMA((1,))],
        compiler_params=pltpu.CompilerParams(vmem_limit_bytes=4 * MIB),
        interpret=INTERPRET,
        name="steps",
    )(back, col)


def edge_kernel(slot_ref, got_ref, other_ref, edge_ref, col_ref, steps_in, steps_hbm, sum_ref, sems):
    my_slot, my_src, above, below = places(slot_ref)
    first = my_src == 0
    last = my_src == SRC_DEVICES - 1
    comes_from = jnp.where(first, above, below)

    @pl.when((first | last) & (comes_from >= 0))
    def _():
        place = comes_from // 2
        same_core = lax.rem(comes_from, 2) == lax.rem(my_slot, 2)
        rim = jnp.where(same_core, got_ref[place].astype(jnp.float32), other_ref[place].astype(jnp.float32))
        sum_ref[...] = edge_ref[...] - LEARN_RATE * dot_t(rim.astype(jnp.bfloat16), col_ref[...])
        start = pl.multiple_of(jnp.where(first, 0, ROWS - HALO), HALO)
        keep = pltpu.make_async_copy(sum_ref, steps_hbm.at[pl.ds(start, HALO)], sems.at[0])
        keep.start()
        keep.wait()


def add_edge(slot_pos, got, other, edge, col, steps):
    return pl.pallas_call(
        edge_kernel,
        out_shape=jax.ShapeDtypeStruct((ROWS, TILE_PX), jnp.float32),
        in_specs=[SCALARS] + [WHOLE] * 4 + [LEFT_THERE],
        out_specs=LEFT_THERE,
        scratch_shapes=[pltpu.VMEM((HALO, TILE_PX), jnp.float32), pltpu.SemaphoreType.DMA((1,))],
        input_output_aliases={5: 0},
        compiler_params=pltpu.CompilerParams(vmem_limit_bytes=4 * MIB),
        interpret=INTERPRET,
        name="edge",
    )(slot_pos, got, other, edge, col, steps)


def pupil_tables(pupil_phase):
    window = pupil_phase[32:96, 32:96]
    real = jnp.where(DISC, jnp.cos(window), 0.0) * SCALE
    imag = jnp.where(DISC, jnp.sin(window), 0.0) * SCALE
    return jnp.stack([jnp.concatenate([real, real], axis=1), jnp.concatenate([-imag, imag], axis=1)])


def own_moments(tile, col, row_table):
    half = jnp.dot(tile, col, preferred_element_type=jnp.float32)
    rows = row_table[HALO : HALO + TILE_PX]
    return lax.dot_general(
        rows, half, (((0,), (0,)), ((), ())), precision=lax.Precision.HIGHEST, preferred_element_type=jnp.float32
    )


def swap_src(value, mask):
    return lax.ppermute(value, "src", [(i, i ^ mask) for i in range(SRC_DEVICES)])


def pair_sources(src_shift, src_weight):
    shifts = jnp.concatenate([src_shift, swap_src(src_shift, 4)], axis=0)
    weights = jnp.concatenate([src_weight, swap_src(src_weight, 4)], axis=0)
    return jnp.concatenate([shifts, weights[:, None]], axis=1)


def all_sources(pair):
    return jnp.concatenate([pair] + [swap_src(pair, mask) for mask in (1, 2, 3)], axis=0)


def per_device(mask_tiles, slot_pos, src_shift, src_weight, pupil_phase, target):
    pair = pair_sources(src_shift, src_weight)
    col = jnp.asarray(COL)
    row_table = lax.optimization_barrier(jnp.asarray(ROW_F32))
    tile = mask_tiles[0]
    got = lax.all_to_all(make_rims(slot_pos, tile, col), "tile", 0, 0, tiled=True)
    pair, col_after, small, grids = lax.optimization_barrier((pair, col, jnp.asarray(SMALL), jnp.asarray(GRIDS)))
    ints = all_sources(pair)
    own = own_moments(tile, col_after, row_table)
    flipped, right_t = flip_tables(small, grids)
    resist, back, sent = make_fields(
        slot_pos, ints, got, own, pupil_tables(pupil_phase), small, right_t, row_table, grids, flipped, target[0]
    )
    cores = [[2 * chip + core for chip in range(TILES // 2)] for core in range(2)]
    got = lax.all_to_all(sent, "tile", 0, 0, tiled=True, axis_index_groups=cores)
    steps, edge = make_steps(back, col)
    got, edge = lax.optimization_barrier((got, edge))
    other = lax.ppermute(got, "tile", [(i, i ^ 1) for i in range(TILES)])
    return (resist[None], add_edge(slot_pos, got, other, edge, col, steps)[None])


def solution(mesh):
    return jax.shard_map(
        per_device,
        mesh=mesh,
        in_specs=(P("tile", None, None), P(), P("src", None), P("src"), P(), P("tile", None, None)),
        out_specs=(P("tile", "src", None), P("tile", "src", None)),
        check_vma=False,
    )
```

```python
import math

import jax
import jax.numpy as jnp
import ml_dtypes
import numpy as np
from jax import lax
from jax.experimental import pallas as pl
from jax.experimental.pallas import tpu as pltpu
from jax.sharding import PartitionSpec as P

TILE_PX = 1024
HALO = 64
EXT_PX = 1152
FREQ = 128
GRID = 128
SOURCES = 16
TILES = 32
SRC_DEVICES = 8
PUPIL_R = 28
ROWS = 128
STEEPNESS = 4.0
THRESHOLD = 0.6
LEARN_RATE = 8.0
SCALE = 1.0 / (FREQ / 2 * math.sqrt(EXT_PX * TILE_PX))
INTERPRET = False
BF16 = ml_dtypes.bfloat16


def split(table):
    high = table.astype(BF16)
    return high, (table - high.astype(np.float64)).astype(BF16)


def half_table(count, period):
    angle = 2 * np.pi * ((np.arange(count)[:, None] * np.arange(64)[None]) % period) / period
    return np.concatenate([np.cos(angle), np.sin(angle)], axis=1)


def unfold_tables():
    even = np.zeros((FREQ, 64))
    odd = np.zeros((FREQ, 64))
    for row, freq in enumerate(range(-64, 64)):
        if freq > -64:
            even[row, abs(freq)] = 1
            odd[row, abs(freq)] = np.sign(freq)
    return even, odd


def coarse_table():
    angle = 2 * np.pi * ((np.arange(GRID)[:, None] * (np.arange(64) - 32)[None]) % GRID) / GRID
    return np.cos(angle), np.sin(angle)


def interpolation(positions):
    apart = positions[:, None] - np.arange(GRID)[None]
    return np.cos(2 * np.pi * apart[:, :, None] * np.arange(-63, 64) / GRID).sum(axis=-1) / GRID


COL = half_table(TILE_PX, TILE_PX).astype(BF16)
ROW = half_table(EXT_PX, EXT_PX)
EVEN, ODD = unfold_tables()
COS_W, SIN_W = coarse_table()
ROW_F32 = ROW.astype(np.float32)
ZERO = np.zeros((FREQ, 64))
UNFOLD = np.concatenate(
    [np.concatenate([EVEN, ZERO], axis=1), np.concatenate([ZERO, ODD], axis=1)], axis=0
)
LEFT_H, LEFT_L = split(np.concatenate([COS_W, SIN_W], axis=0))
RIGHT = np.concatenate(
    split(
        np.concatenate(
            [np.concatenate([COS_W.T, SIN_W.T], axis=1), np.concatenate([-SIN_W.T, COS_W.T], axis=1)], axis=0
        )
    ),
    axis=0,
)
LEFT_T = np.concatenate(split(np.concatenate([COS_W.T, SIN_W.T], axis=0)), axis=0)
RIM = np.concatenate(split(np.concatenate([ROW[:HALO], ROW[EXT_PX - HALO :]], axis=0).T), axis=1)
SMALL = np.concatenate(
    [
        UNFOLD.astype(BF16),
        np.concatenate([LEFT_H, LEFT_H, LEFT_L, np.zeros_like(LEFT_L)], axis=1),
        RIGHT,
        LEFT_T,
        np.concatenate([RIM, UNFOLD.T.astype(BF16)], axis=0),
        RIGHT.T,
    ],
    axis=1,
)
ROWS_Y = (HALO + np.arange(TILE_PX)) / 9.0
GRIDS = np.concatenate(split(interpolation(ROWS_Y)) + split(interpolation(np.arange(TILE_PX) / 8.0)), axis=1)
DISC = (np.arange(64)[:, None] - 32) ** 2 + (np.arange(64)[None] - 32) ** 2 <= PUPIL_R * PUPIL_R


def dot(left, right):
    return jnp.dot(left, right, preferred_element_type=jnp.float32)


def dot_t(left, right):
    return lax.dot_general(left, right, (((1,), (1,)), ((), ())), preferred_element_type=jnp.float32)


def halves(value):
    high = value.astype(jnp.bfloat16)
    return high, (value - high.astype(jnp.float32)).astype(jnp.bfloat16)


def low_lanes(shape):
    return lax.broadcasted_iota(jnp.int32, shape, 1) < 64


def places(slot_ref):
    my_slot = lax.axis_index("tile")
    my_position = slot_ref[my_slot]
    above = jnp.int32(-1)
    below = jnp.int32(-1)
    for slot in range(TILES):
        position = slot_ref[slot]
        above = jnp.where(position == my_position - 1, slot, above)
        below = jnp.where(position == my_position + 1, slot, below)
    return my_slot, lax.axis_index("src"), above, below


def rims_kernel(
    slot_ref, shift_ref, weight_ref, tile_hbm, col_hbm, sent_hbm, ints_hbm, rows_ref, col_ref, rims_ref, ints_ref, sems
):
    copies = [
        pltpu.make_async_copy(col_hbm, col_ref, sems.at[0]),
        pltpu.make_async_copy(tile_hbm.at[pl.ds(0, HALO)], rows_ref.at[pl.ds(0, HALO)], sems.at[1]),
        pltpu.make_async_copy(
            tile_hbm.at[pl.ds(TILE_PX - HALO, HALO)], rows_ref.at[pl.ds(HALO, HALO)], sems.at[2]
        ),
    ]
    for copy in copies:
        copy.start()
    my_slot, my_src, above, below = places(slot_ref)
    row = lax.broadcasted_iota(jnp.int32, ints_ref.shape, 0) - 2 * my_src
    lane = lax.broadcasted_iota(jnp.int32, ints_ref.shape, 1)
    table = jnp.zeros(ints_ref.shape, jnp.int32)
    for source in range(2):
        for place, value in enumerate((shift_ref[source, 0], shift_ref[source, 1], weight_ref[source])):
            table = jnp.where((row == source) & (lane == place), value, table)
    ints_ref[...] = table
    ints_keep = pltpu.make_async_copy(ints_ref, ints_hbm, sems.at[5])
    ints_keep.start()
    for copy in copies:
        copy.wait()
    rims_ref[...] = dot(rows_ref[...], col_ref[...]).astype(jnp.bfloat16).reshape(2, HALO, 128)

    for number, slot in enumerate((above, below)):

        @pl.when(slot >= 0)
        def _():
            pltpu.make_async_copy(rims_ref.at[number], sent_hbm.at[slot], sems.at[3 + number]).start()

    for number, slot in enumerate((above, below)):

        @pl.when(slot >= 0)
        def _():
            pltpu.make_async_copy(rims_ref.at[number], sent_hbm.at[slot], sems.at[3 + number]).wait()

    ints_keep.wait()


SCALARS = pl.BlockSpec(memory_space=pltpu.SMEM)
WHOLE = pl.BlockSpec(memory_space=pltpu.VMEM)
LEFT_THERE = pl.BlockSpec(memory_space=pltpu.MemorySpace.HBM)
MIB = 1024 * 1024
ALL_VMEM = 63_000_000
FIELDS_VMEM = 54_000_000


def make_rims(slot_pos, src_shift, src_weight, tile, col):
    return pl.pallas_call(
        rims_kernel,
        out_shape=(
            jax.ShapeDtypeStruct((TILES, HALO, 128), jnp.bfloat16),
            jax.ShapeDtypeStruct((SOURCES, 128), jnp.int32),
        ),
        in_specs=[SCALARS, SCALARS, SCALARS, LEFT_THERE, LEFT_THERE],
        out_specs=[LEFT_THERE, LEFT_THERE],
        scratch_shapes=[
            pltpu.VMEM((2 * HALO, TILE_PX), jnp.bfloat16),
            pltpu.VMEM((TILE_PX, 128), jnp.bfloat16),
            pltpu.VMEM((2, HALO, 128), jnp.bfloat16),
            pltpu.VMEM((SOURCES, 128), jnp.int32),
            pltpu.SemaphoreType.DMA((6,)),
        ],
        compiler_params=pltpu.CompilerParams(vmem_limit_bytes=ALL_VMEM),
        interpret=INTERPRET,
        name="rims",
    )(slot_pos, src_shift, src_weight, tile, col)


def prep_kernel(grids_hbm, flipped_hbm, grids_ref, flipped_ref, sems):
    fetch = pltpu.make_async_copy(grids_hbm, grids_ref, sems.at[0])
    fetch.start()
    fetch.wait()
    flipped_ref[...] = grids_ref[...].T
    keep = pltpu.make_async_copy(flipped_ref, flipped_hbm, sems.at[1])
    keep.start()
    keep.wait()


def flip_tables(grids):
    return pl.pallas_call(
        prep_kernel,
        out_shape=jax.ShapeDtypeStruct(GRIDS.shape[::-1], jnp.bfloat16),
        in_specs=[LEFT_THERE],
        out_specs=LEFT_THERE,
        scratch_shapes=[
            pltpu.VMEM(GRIDS.shape, jnp.bfloat16),
            pltpu.VMEM(GRIDS.shape[::-1], jnp.bfloat16),
            pltpu.SemaphoreType.DMA((2,)),
        ],
        compiler_params=pltpu.CompilerParams(vmem_limit_bytes=ALL_VMEM),
        interpret=INTERPRET,
        name="prep",
    )(grids)


def fields_kernel(
    slot_ref, ints_ref, got_ref, own_ref, pupil_ref, small_ref, row_ref, grids_hbm, flipped_hbm, target_hbm,
    resist_hbm, back_ref, sent_hbm,
    edge_ref, grids_ref, flipped_ref, target_ref, resist_ref, spec_ref, field_ref, fold_ref, grad_ref, sems,
):
    fetches = [
        pltpu.make_async_copy(source, target, sems.at[number])
        for number, (source, target) in enumerate(
            [(grids_hbm.at[:, pl.ds(0, 256)], grids_ref.at[:, pl.ds(0, 256)]), (flipped_hbm.at[pl.ds(256, 128)], flipped_ref.at[pl.ds(256, 128)])]
            + [(target_hbm.at[pl.ds(256 * part, 256)], target_ref.at[pl.ds(256 * part, 256)]) for part in range(4)]
            + [(grids_hbm.at[:, pl.ds(256, 256)], grids_ref.at[:, pl.ds(256, 256)]), (flipped_hbm.at[pl.ds(0, 256)], flipped_ref.at[pl.ds(0, 256)])]
        )
    ]
    fetches = [fetches[number] for number in (0, 1, 6, 2, 3, 4, 5, 7)]
    for fetch in fetches:
        fetch.start()
    my_slot, my_src, above, below = places(slot_ref)
    unfold = small_ref[:, 0:128]
    left = small_ref[:, 128:320]
    right = small_ref[:, 384:640]
    left_t = small_ref[:, 640:768]
    rim_table = small_ref[:128, 768:1024]
    unfold_t = small_ref[128:, 768:1024]
    lanes = unfold[:128] + unfold[128:]
    lanes2 = jnp.concatenate([lanes, lanes], axis=1)
    low = low_lanes((128, 128))
    low_w = low_lanes((64, 128))
    up = jnp.where(above >= 0, got_ref[jnp.maximum(above, 0)].astype(jnp.float32), 0.0)
    down = jnp.where(below >= 0, got_ref[jnp.maximum(below, 0)].astype(jnp.float32), 0.0)
    rims = jnp.concatenate([up, down], axis=0).astype(jnp.bfloat16)
    moments = own_ref[...] + dot(rim_table, jnp.concatenate([rims, rims], axis=0))
    half = dot(jnp.concatenate([unfold, unfold], axis=1), jnp.concatenate(halves(moments), axis=0))
    by_cos, by_sin = half[:FREQ], half[FREQ:]
    spec_ref[0] = dot_t(jnp.concatenate(halves(jnp.where(low, by_cos, -by_sin)), axis=1), lanes2)
    spec_ref[1] = dot_t(jnp.concatenate(halves(jnp.where(low, -by_sin, -by_cos)), axis=1), lanes2)
    coarse = jnp.zeros((GRID, GRID), jnp.float32)
    for source in range(SOURCES):
        shift_a = ints_ref[source, 0]
        shift_b = ints_ref[source, 1]
        rows = pl.ds(32 - shift_a, 64)
        spec_re = spec_ref[0, rows, :]
        spec_im = spec_ref[1, rows, :]
        near = lax.rem(96 + shift_b, 128)
        far = 32 + shift_b
        window = jnp.where(low_w, pltpu.roll(spec_re, near, 1), pltpu.roll(spec_im, far, 1))
        amp = pupil_ref[0] * window + pupil_ref[1] * pltpu.roll(window, 64, 1)
        amp_h, amp_l = halves(amp)
        both = dot(left, jnp.concatenate([amp_h, amp_l, amp_h], axis=0))
        swapped = pltpu.roll(both[GRID:], 64, 1)
        line = both[:GRID] + jnp.where(low, -swapped, swapped)
        line_h, line_l = halves(line)
        field = dot(jnp.concatenate([line_h, line_h], axis=1), right) + dot(line_l, right[:128])
        field_ref[source] = field
        weight = ints_ref[source, 2].astype(jnp.float32) * (1.0 / (4.0 * SOURCES))
        squared = field * field
        coarse = coarse + weight * (squared[:, :GRID] + squared[:, GRID:])
    coarse_h, coarse_l = halves(coarse)
    coarse_hh = jnp.concatenate([coarse_h, coarse_h], axis=0)
    for fetch in fetches[:3]:
        fetch.wait()
    grid_x = grids_ref[:, 256:512]
    grid_xhh = jnp.concatenate([flipped_ref[256:384, :], flipped_ref[256:384, :]], axis=0)
    chunk = 256
    for place in range(TILE_PX // chunk):
        rows = pl.ds(place * chunk, chunk)
        rows_y = dot(grids_ref[rows, 0:256], coarse_hh) + dot(grids_ref[rows, 0:128], coarse_l)
        rows_h, rows_l = halves(rows_y)
        intensity = dot(jnp.concatenate([rows_h, rows_l], axis=1), grid_xhh)
        resist = jax.nn.sigmoid(STEEPNESS * (intensity - THRESHOLD))
        resist_ref[rows, :] = resist
        fetches[3 + place].wait()
        wanted = target_ref[rows, :].astype(jnp.float32)
        adjoint = ((2.0 * STEEPNESS) * (resist - wanted) * resist * (1.0 - resist)).astype(jnp.bfloat16)
        folded = dot(adjoint, grid_x)
        fold_ref[rows, :] = jnp.concatenate(halves(folded[:, :GRID] + folded[:, GRID:]), axis=1)
    mine = pl.multiple_of(my_src * ROWS, ROWS)
    keep = pltpu.make_async_copy(resist_ref.at[pl.ds(mine, ROWS)], resist_hbm, sems.at[8])
    keep.start()
    fetches[7].wait()
    adjoint4 = dot(flipped_ref[0:256, :], fold_ref[...])
    adjoint2 = adjoint4[:GRID] + adjoint4[GRID:]
    coarse_adjoint = 2.0 * (adjoint2[:, :GRID] + adjoint2[:, GRID:])
    right_t = small_ref[:, 1024:1280]
    grad_ref[...] = jnp.zeros(grad_ref.shape, jnp.float32)
    for source in range(SOURCES):
        shift_a = ints_ref[source, 0]
        shift_b = ints_ref[source, 1]
        weight = ints_ref[source, 2].astype(jnp.float32) * (1.0 / (4.0 * SOURCES))
        weighted = weight * coarse_adjoint
        dfield_h, dfield_l = halves(field_ref[source] * jnp.concatenate([weighted, weighted], axis=1))
        dline2 = dot(dfield_h, right_t)
        dline = dline2[:, :128] + dline2[:, 128:] + dot(dfield_l, right_t[:, :128])
        damp4 = dot(left_t, jnp.concatenate(halves(dline), axis=1))
        damp2 = damp4[:128] + damp4[128:]
        damp1 = damp2[:, :128] + damp2[:, 128:]
        swapped = pltpu.roll(damp1[64:], 64, 1)
        damp = damp1[:64] + jnp.where(low_w, swapped, -swapped)
        grad = pupil_ref[0] * damp - pupil_ref[1] * pltpu.roll(damp, 64, 1)
        rows = pl.ds(32 - shift_a, 64)
        grad_ref[0, rows, :] += pltpu.roll(jnp.where(low_w, grad, 0.0), 32 - shift_b, 1)
        grad_ref[1, rows, :] += pltpu.roll(jnp.where(low_w, 0.0, grad), lax.rem(96 - shift_b, 128), 1)
    grads = jnp.concatenate([grad_ref[0], grad_ref[1]], axis=0)
    folded = dot(jnp.concatenate(halves(grads), axis=1), jnp.concatenate([lanes, lanes], axis=0))
    fold_re, fold_im = folded[:FREQ], folded[FREQ:]
    packed = jnp.concatenate(
        [jnp.where(low, fold_re, -fold_im), jnp.where(low, -fold_im, -fold_re)], axis=0
    )
    packed = dot(jnp.concatenate([unfold_t, unfold_t], axis=1), jnp.concatenate(halves(packed), axis=0))
    first = my_src == 0
    edge_rows = row_ref[pl.ds(pl.multiple_of(jnp.where(first, EXT_PX - HALO, 0), HALO), HALO), :]
    mine_rows = row_ref[pl.ds(pl.multiple_of(HALO + my_src * ROWS, HALO), ROWS), :]
    tables = jnp.concatenate([edge_rows, mine_rows], axis=0)
    back = jnp.dot(tables, packed, precision=lax.Precision.HIGHEST, preferred_element_type=jnp.float32)
    goes_to = jnp.where(first, below, above)

    @pl.when(goes_to >= 0)
    def _():
        edge_ref[...] = back[:HALO].astype(jnp.bfloat16)
        send = pltpu.make_async_copy(edge_ref, sent_hbm.at[goes_to // 2], sems.at[9])
        send.start()
        send.wait()

    back_ref[...] = back[HALO:]
    keep.wait()


def make_fields(slot_pos, ints, *arrays):
    return pl.pallas_call(
        fields_kernel,
        out_shape=(
            jax.ShapeDtypeStruct((ROWS, TILE_PX), jnp.float32),
            jax.ShapeDtypeStruct((ROWS, 128), jnp.float32),
            jax.ShapeDtypeStruct((TILES // 2, HALO, 128), jnp.bfloat16),
        ),
        in_specs=[SCALARS, SCALARS] + [WHOLE] * 5 + [LEFT_THERE] * 3,
        out_specs=[LEFT_THERE, WHOLE, LEFT_THERE],
        scratch_shapes=[
            pltpu.VMEM((HALO, 128), jnp.bfloat16),
            pltpu.VMEM(GRIDS.shape, jnp.bfloat16),
            pltpu.VMEM(GRIDS.shape[::-1], jnp.bfloat16),
            pltpu.VMEM((TILE_PX, TILE_PX), jnp.bfloat16),
            pltpu.VMEM((TILE_PX, TILE_PX), jnp.float32),
            pltpu.VMEM((2, FREQ, FREQ), jnp.float32),
            pltpu.VMEM((SOURCES, GRID, 2 * GRID), jnp.float32),
            pltpu.VMEM((TILE_PX, 2 * GRID), jnp.bfloat16),
            pltpu.VMEM((2, FREQ, FREQ), jnp.float32),
            pltpu.SemaphoreType.DMA((10,)),
        ],
        compiler_params=pltpu.CompilerParams(vmem_limit_bytes=FIELDS_VMEM),
        interpret=INTERPRET,
        name="fields",
    )(slot_pos, ints, *arrays)


def steps_kernel(back_ref, col_ref, steps_hbm, edge_ref, steps_ref, sems):
    my_src = lax.axis_index("src")
    high, low = halves(-LEARN_RATE * back_ref[...])
    steps_ref[...] = dot_t(high, col_ref[...]) + dot_t(low, col_ref[...])
    keep = pltpu.make_async_copy(steps_ref, steps_hbm, sems.at[0])
    keep.start()
    at_end = my_src == SRC_DEVICES - 1
    edge_ref[...] = jnp.where(at_end, steps_ref[ROWS - HALO :, :], steps_ref[:HALO, :])
    keep.wait()


def make_steps(back, col):
    return pl.pallas_call(
        steps_kernel,
        out_shape=(
            jax.ShapeDtypeStruct((ROWS, TILE_PX), jnp.float32),
            jax.ShapeDtypeStruct((HALO, TILE_PX), jnp.float32),
        ),
        in_specs=[WHOLE, WHOLE],
        out_specs=[LEFT_THERE, WHOLE],
        scratch_shapes=[pltpu.VMEM((ROWS, TILE_PX), jnp.float32), pltpu.SemaphoreType.DMA((1,))],
        compiler_params=pltpu.CompilerParams(vmem_limit_bytes=4 * MIB),
        interpret=INTERPRET,
        name="steps",
    )(back, col)


def edge_kernel(slot_ref, got_ref, other_ref, edge_ref, col_ref, steps_in, steps_hbm, sum_ref, sems):
    my_slot, my_src, above, below = places(slot_ref)
    first = my_src == 0
    last = my_src == SRC_DEVICES - 1
    comes_from = jnp.where(first, above, below)

    @pl.when((first | last) & (comes_from >= 0))
    def _():
        place = comes_from // 2
        same_core = lax.rem(comes_from, 2) == lax.rem(my_slot, 2)
        rim = jnp.where(same_core, got_ref[place].astype(jnp.float32), other_ref[place].astype(jnp.float32))
        sum_ref[...] = edge_ref[...] - LEARN_RATE * dot_t(rim.astype(jnp.bfloat16), col_ref[...])
        start = pl.multiple_of(jnp.where(first, 0, ROWS - HALO), HALO)
        keep = pltpu.make_async_copy(sum_ref, steps_hbm.at[pl.ds(start, HALO)], sems.at[0])
        keep.start()
        keep.wait()


def add_edge(slot_pos, got, other, edge, col, steps):
    return pl.pallas_call(
        edge_kernel,
        out_shape=jax.ShapeDtypeStruct((ROWS, TILE_PX), jnp.float32),
        in_specs=[SCALARS] + [WHOLE] * 4 + [LEFT_THERE],
        out_specs=LEFT_THERE,
        scratch_shapes=[pltpu.VMEM((HALO, TILE_PX), jnp.float32), pltpu.SemaphoreType.DMA((1,))],
        input_output_aliases={5: 0},
        compiler_params=pltpu.CompilerParams(vmem_limit_bytes=4 * MIB),
        interpret=INTERPRET,
        name="edge",
    )(slot_pos, got, other, edge, col, steps)


def pupil_tables(pupil_phase):
    window = pupil_phase[32:96, 32:96]
    real = jnp.where(DISC, jnp.cos(window), 0.0) * SCALE
    imag = jnp.where(DISC, jnp.sin(window), 0.0) * SCALE
    return jnp.stack([jnp.concatenate([real, real], axis=1), jnp.concatenate([-imag, imag], axis=1)])


def own_moments(tile, col, row_table):
    half = jnp.dot(tile, col, preferred_element_type=jnp.float32)
    rows = row_table[HALO : HALO + TILE_PX]
    return lax.dot_general(
        rows, half, (((0,), (0,)), ((), ())), precision=lax.Precision.HIGHEST, preferred_element_type=jnp.float32
    )


def swap_src(value, mask):
    return lax.ppermute(value, "src", [(i, i ^ mask) for i in range(SRC_DEVICES)])


def per_device(mask_tiles, slot_pos, src_shift, src_weight, pupil_phase, target):
    col = jnp.asarray(COL)
    row_table = lax.optimization_barrier(jnp.asarray(ROW_F32))
    tile = mask_tiles[0]
    sent, ints = make_rims(slot_pos, src_shift, src_weight, tile, col)
    ints = ints + swap_src(ints, 4)
    got = lax.all_to_all(sent, "tile", 0, 0, tiled=True)
    ints = ints + swap_src(ints, 1) + swap_src(ints, 2) + swap_src(ints, 3)
    small = jnp.asarray(SMALL)
    grids = jnp.asarray(GRIDS)
    own = own_moments(tile, col, row_table)
    flipped = flip_tables(grids)
    resist, back, sent = make_fields(
        slot_pos, ints, got, own, pupil_tables(pupil_phase), small, row_table, grids, flipped, target[0]
    )
    cores = [[2 * chip + core for chip in range(TILES // 2)] for core in range(2)]
    got = lax.all_to_all(sent, "tile", 0, 0, tiled=True, axis_index_groups=cores)
    steps, edge = make_steps(back, col)
    got, edge = lax.optimization_barrier((got, edge))
    other = lax.ppermute(got, "tile", [(i, i ^ 1) for i in range(TILES)])
    return (resist[None], add_edge(slot_pos, got, other, edge, col, steps)[None])


def solution(mesh):
    return jax.shard_map(
        per_device,
        mesh=mesh,
        in_specs=(P("tile", None, None), P(), P("src", None), P("src"), P(), P("tile", None, None)),
        out_specs=(P("tile", "src", None), P("tile", "src", None)),
        check_vma=False,
    )
```

```python
import math

import jax
import jax.numpy as jnp
import ml_dtypes
import numpy as np
from jax import lax
from jax.experimental import pallas as pl
from jax.experimental.pallas import tpu as pltpu
from jax.sharding import PartitionSpec as P

TILE_PX = 1024
HALO = 64
EXT_PX = 1152
FREQ = 128
GRID = 128
SOURCES = 16
TILES = 32
SRC_DEVICES = 8
PUPIL_R = 28
ROWS = 128
STEEPNESS = 4.0
THRESHOLD = 0.6
LEARN_RATE = 8.0
SCALE = 1.0 / (FREQ / 2 * math.sqrt(EXT_PX * TILE_PX))
INTERPRET = False
BF16 = ml_dtypes.bfloat16


def split(table):
    high = table.astype(BF16)
    return high, (table - high.astype(np.float64)).astype(BF16)


def half_table(count, period):
    angle = 2 * np.pi * ((np.arange(count)[:, None] * np.arange(64)[None]) % period) / period
    return np.concatenate([np.cos(angle), np.sin(angle)], axis=1)


def unfold_tables():
    even = np.zeros((FREQ, 64))
    odd = np.zeros((FREQ, 64))
    for row, freq in enumerate(range(-64, 64)):
        if freq > -64:
            even[row, abs(freq)] = 1
            odd[row, abs(freq)] = np.sign(freq)
    return even, odd


def coarse_table():
    angle = 2 * np.pi * ((np.arange(GRID)[:, None] * (np.arange(64) - 32)[None]) % GRID) / GRID
    return np.cos(angle), np.sin(angle)


def interpolation(positions):
    apart = positions[:, None] - np.arange(GRID)[None]
    return np.cos(2 * np.pi * apart[:, :, None] * np.arange(-63, 64) / GRID).sum(axis=-1) / GRID


COL = half_table(TILE_PX, TILE_PX).astype(BF16)
ROW = half_table(EXT_PX, EXT_PX)
EVEN, ODD = unfold_tables()
COS_W, SIN_W = coarse_table()
ROW_F32 = ROW.astype(np.float32)
ZERO = np.zeros((FREQ, 64))
UNFOLD = np.concatenate(
    [np.concatenate([EVEN, ZERO], axis=1), np.concatenate([ZERO, ODD], axis=1)], axis=0
)
LEFT_H, LEFT_L = split(np.concatenate([COS_W, SIN_W], axis=0))
RIGHT = np.concatenate(
    split(
        np.concatenate(
            [np.concatenate([COS_W.T, SIN_W.T], axis=1), np.concatenate([-SIN_W.T, COS_W.T], axis=1)], axis=0
        )
    ),
    axis=0,
)
LEFT_T = np.concatenate(split(np.concatenate([COS_W.T, SIN_W.T], axis=0)), axis=0)
RIM = np.concatenate(split(np.concatenate([ROW[:HALO], ROW[EXT_PX - HALO :]], axis=0).T), axis=1)
LANES = np.concatenate([EVEN, ODD], axis=1)
SMALL = np.concatenate(
    [
        UNFOLD.astype(BF16),
        np.concatenate([LEFT_H, LEFT_H, LEFT_L, np.zeros_like(LEFT_L)], axis=1),
        RIGHT,
        LEFT_T,
        np.concatenate([RIM, UNFOLD.T.astype(BF16)], axis=0),
        np.concatenate([LANES, np.zeros_like(LANES)], axis=0).astype(BF16),
    ],
    axis=1,
)
ROWS_Y = (HALO + np.arange(TILE_PX)) / 9.0
GRIDS = np.concatenate(split(interpolation(ROWS_Y)) + split(interpolation(np.arange(TILE_PX) / 8.0)), axis=1)
DISC = (np.arange(64)[:, None] - 32) ** 2 + (np.arange(64)[None] - 32) ** 2 <= PUPIL_R * PUPIL_R


def dot(left, right):
    return jnp.dot(left, right, preferred_element_type=jnp.float32)


def dot_t(left, right):
    return lax.dot_general(left, right, (((1,), (1,)), ((), ())), preferred_element_type=jnp.float32)


def halves(value):
    high = value.astype(jnp.bfloat16)
    return high, (value - high.astype(jnp.float32)).astype(jnp.bfloat16)


def low_lanes(shape):
    return lax.broadcasted_iota(jnp.int32, shape, 1) < 64


def places(slot_ref):
    my_slot = lax.axis_index("tile")
    my_position = slot_ref[my_slot]
    above = jnp.int32(-1)
    below = jnp.int32(-1)
    for slot in range(TILES):
        position = slot_ref[slot]
        above = jnp.where(position == my_position - 1, slot, above)
        below = jnp.where(position == my_position + 1, slot, below)
    return my_slot, lax.axis_index("src"), above, below


def pack_kernel(shift_ref, weight_ref, ints_ref):
    row = lax.broadcasted_iota(jnp.int32, ints_ref.shape, 0) - 2 * lax.axis_index("src")
    lane = lax.broadcasted_iota(jnp.int32, ints_ref.shape, 1)
    table = jnp.zeros(ints_ref.shape, jnp.int32)
    for source in range(2):
        for place, value in enumerate((shift_ref[source, 0], shift_ref[source, 1], weight_ref[source])):
            table = jnp.where((row == source) & (lane == place), value, table)
    ints_ref[...] = table


def rims_kernel(slot_ref, tile_hbm, col_hbm, sent_hbm, rows_ref, col_ref, rims_ref, sems):
    copies = [
        pltpu.make_async_copy(col_hbm, col_ref, sems.at[0]),
        pltpu.make_async_copy(tile_hbm.at[pl.ds(0, HALO)], rows_ref.at[pl.ds(0, HALO)], sems.at[1]),
        pltpu.make_async_copy(
            tile_hbm.at[pl.ds(TILE_PX - HALO, HALO)], rows_ref.at[pl.ds(HALO, HALO)], sems.at[2]
        ),
    ]
    for copy in copies:
        copy.start()
    my_slot, my_src, above, below = places(slot_ref)
    for copy in copies:
        copy.wait()
    rims_ref[...] = dot(rows_ref[...], col_ref[...]).astype(jnp.bfloat16).reshape(2, HALO, 128)

    for number, slot in enumerate((above, below)):

        @pl.when(slot >= 0)
        def _():
            pltpu.make_async_copy(rims_ref.at[number], sent_hbm.at[slot], sems.at[3 + number]).start()

    for number, slot in enumerate((above, below)):

        @pl.when(slot >= 0)
        def _():
            pltpu.make_async_copy(rims_ref.at[number], sent_hbm.at[slot], sems.at[3 + number]).wait()


SCALARS = pl.BlockSpec(memory_space=pltpu.SMEM)
WHOLE = pl.BlockSpec(memory_space=pltpu.VMEM)
LEFT_THERE = pl.BlockSpec(memory_space=pltpu.MemorySpace.HBM)
MIB = 1024 * 1024
ALL_VMEM = 63_000_000
FIELDS_VMEM = 54_000_000


def pack_sources(src_shift, src_weight):
    return pl.pallas_call(
        pack_kernel,
        out_shape=jax.ShapeDtypeStruct((SOURCES, 128), jnp.int32),
        in_specs=[SCALARS, SCALARS],
        out_specs=WHOLE,
        compiler_params=pltpu.CompilerParams(vmem_limit_bytes=4 * MIB),
        interpret=INTERPRET,
        name="pack",
    )(src_shift, src_weight)


def make_rims(slot_pos, tile, col):
    return pl.pallas_call(
        rims_kernel,
        out_shape=jax.ShapeDtypeStruct((TILES, HALO, 128), jnp.bfloat16),
        in_specs=[SCALARS, LEFT_THERE, LEFT_THERE],
        out_specs=LEFT_THERE,
        scratch_shapes=[
            pltpu.VMEM((2 * HALO, TILE_PX), jnp.bfloat16),
            pltpu.VMEM((TILE_PX, 128), jnp.bfloat16),
            pltpu.VMEM((2, HALO, 128), jnp.bfloat16),
            pltpu.SemaphoreType.DMA((5,)),
        ],
        compiler_params=pltpu.CompilerParams(vmem_limit_bytes=ALL_VMEM),
        interpret=INTERPRET,
        name="rims",
    )(slot_pos, tile, col)


def prep_kernel(small_hbm, grids_hbm, flipped_hbm, right_t_hbm, small_ref, grids_ref, flipped_ref, right_t_ref, sems):
    fetches = [
        pltpu.make_async_copy(grids_hbm, grids_ref, sems.at[0]),
        pltpu.make_async_copy(small_hbm.at[:, pl.ds(384, 256)], small_ref, sems.at[1]),
    ]
    keeps = [
        pltpu.make_async_copy(flipped_ref, flipped_hbm, sems.at[2]),
        pltpu.make_async_copy(right_t_ref, right_t_hbm, sems.at[3]),
    ]
    for fetch in fetches:
        fetch.start()
    fetches[0].wait()
    flipped_ref[...] = grids_ref[...].T
    keeps[0].start()
    fetches[1].wait()
    right_t_ref[...] = small_ref[...].T
    keeps[1].start()
    for keep in keeps:
        keep.wait()


def flip_tables(small, grids):
    return pl.pallas_call(
        prep_kernel,
        out_shape=(
            jax.ShapeDtypeStruct(GRIDS.shape[::-1], jnp.bfloat16),
            jax.ShapeDtypeStruct((256, 256), jnp.bfloat16),
        ),
        in_specs=[LEFT_THERE] * 2,
        out_specs=[LEFT_THERE] * 2,
        scratch_shapes=[
            pltpu.VMEM((256, 256), jnp.bfloat16),
            pltpu.VMEM(GRIDS.shape, jnp.bfloat16),
            pltpu.VMEM(GRIDS.shape[::-1], jnp.bfloat16),
            pltpu.VMEM((256, 256), jnp.bfloat16),
            pltpu.SemaphoreType.DMA((4,)),
        ],
        compiler_params=pltpu.CompilerParams(vmem_limit_bytes=ALL_VMEM),
        interpret=INTERPRET,
        name="prep",
    )(small, grids)


def fields_kernel(
    slot_ref, ints_ref, got_ref, own_ref, pupil_ref, small_ref, right_t_ref, row_ref, grids_hbm, flipped_hbm, target_hbm,
    resist_hbm, back_ref, sent_hbm,
    edge_ref, grids_ref, flipped_ref, target_ref, resist_ref, spec_ref, field_ref, fold_ref, grad_ref, sems,
):
    fetches = [
        pltpu.make_async_copy(source, target, sems.at[number])
        for number, (source, target) in enumerate(
            [(grids_hbm.at[:, pl.ds(0, 256)], grids_ref.at[:, pl.ds(0, 256)]), (flipped_hbm.at[pl.ds(256, 128)], flipped_ref.at[pl.ds(256, 128)])]
            + [(target_hbm.at[pl.ds(256 * part, 256)], target_ref.at[pl.ds(256 * part, 256)]) for part in range(4)]
            + [(grids_hbm.at[:, pl.ds(256, 256)], grids_ref.at[:, pl.ds(256, 256)]), (flipped_hbm.at[pl.ds(0, 256)], flipped_ref.at[pl.ds(0, 256)])]
        )
    ]
    fetches = [fetches[number] for number in (0, 1, 6, 2, 3, 4, 5, 7)]
    for fetch in fetches:
        fetch.start()
    my_slot, my_src, above, below = places(slot_ref)
    unfold = small_ref[:, 0:128]
    left = small_ref[:, 128:320]
    right = small_ref[:, 384:640]
    left_t = small_ref[:, 640:768]
    rim_table = small_ref[:128, 768:1024]
    unfold_t = small_ref[128:, 768:1024]
    lanes = small_ref[:128, 1024:1152]
    lanes2 = jnp.concatenate([lanes, lanes], axis=1)
    low = low_lanes((128, 128))
    low_w = low_lanes((64, 128))
    up = jnp.where(above >= 0, got_ref[jnp.maximum(above, 0)].astype(jnp.float32), 0.0)
    down = jnp.where(below >= 0, got_ref[jnp.maximum(below, 0)].astype(jnp.float32), 0.0)
    rims = jnp.concatenate([up, down], axis=0).astype(jnp.bfloat16)
    moments = own_ref[...] + dot(rim_table, jnp.concatenate([rims, rims], axis=0))
    half = dot(jnp.concatenate([unfold, unfold], axis=1), jnp.concatenate(halves(moments), axis=0))
    by_cos, by_sin = half[:FREQ], half[FREQ:]
    spec_ref[0] = dot_t(jnp.concatenate(halves(jnp.where(low, by_cos, -by_sin)), axis=1), lanes2)
    spec_ref[1] = dot_t(jnp.concatenate(halves(jnp.where(low, -by_sin, -by_cos)), axis=1), lanes2)
    coarse = jnp.zeros((GRID, GRID), jnp.float32)
    for source in range(SOURCES):
        shift_a = ints_ref[source, 0]
        shift_b = ints_ref[source, 1]
        rows = pl.ds(32 - shift_a, 64)
        spec_re = spec_ref[0, rows, :]
        spec_im = spec_ref[1, rows, :]
        near = lax.rem(96 + shift_b, 128)
        far = 32 + shift_b
        window = jnp.where(low_w, pltpu.roll(spec_re, near, 1), pltpu.roll(spec_im, far, 1))
        amp = pupil_ref[0] * window + pupil_ref[1] * pltpu.roll(window, 64, 1)
        amp_h, amp_l = halves(amp)
        both = dot(left, jnp.concatenate([amp_h, amp_l, amp_h], axis=0))
        swapped = pltpu.roll(both[GRID:], 64, 1)
        line = both[:GRID] + jnp.where(low, -swapped, swapped)
        line_h, line_l = halves(line)
        field = dot(jnp.concatenate([line_h, line_h], axis=1), right) + dot(line_l, right[:128])
        field_ref[source] = field
        weight = ints_ref[source, 2].astype(jnp.float32) * (1.0 / (4.0 * SOURCES))
        squared = field * field
        coarse = coarse + weight * (squared[:, :GRID] + squared[:, GRID:])
    coarse_h, coarse_l = halves(coarse)
    coarse_hh = jnp.concatenate([coarse_h, coarse_h], axis=0)
    for fetch in fetches[:3]:
        fetch.wait()
    grid_x = grids_ref[:, 256:512]
    grid_xhh = jnp.concatenate([flipped_ref[256:384, :], flipped_ref[256:384, :]], axis=0)
    chunk = 256
    for place in range(TILE_PX // chunk):
        rows = pl.ds(place * chunk, chunk)
        rows_y = dot(grids_ref[rows, 0:256], coarse_hh) + dot(grids_ref[rows, 0:128], coarse_l)
        rows_h, rows_l = halves(rows_y)
        intensity = dot(jnp.concatenate([rows_h, rows_l], axis=1), grid_xhh)
        resist = jax.nn.sigmoid(STEEPNESS * (intensity - THRESHOLD))
        resist_ref[rows, :] = resist
        fetches[3 + place].wait()
        wanted = target_ref[rows, :].astype(jnp.float32)
        adjoint = ((2.0 * STEEPNESS) * (resist - wanted) * resist * (1.0 - resist)).astype(jnp.bfloat16)
        folded = dot(adjoint, grid_x)
        fold_ref[rows, :] = jnp.concatenate(halves(folded[:, :GRID] + folded[:, GRID:]), axis=1)
    mine = pl.multiple_of(my_src * ROWS, ROWS)
    keep = pltpu.make_async_copy(resist_ref.at[pl.ds(mine, ROWS)], resist_hbm, sems.at[8])
    keep.start()
    fetches[7].wait()
    adjoint4 = dot(flipped_ref[0:256, :], fold_ref[...])
    adjoint2 = adjoint4[:GRID] + adjoint4[GRID:]
    coarse_adjoint = 2.0 * (adjoint2[:, :GRID] + adjoint2[:, GRID:])
    right_t = right_t_ref[...]
    grad_ref[...] = jnp.zeros(grad_ref.shape, jnp.float32)
    for source in range(SOURCES):
        shift_a = ints_ref[source, 0]
        shift_b = ints_ref[source, 1]
        weight = ints_ref[source, 2].astype(jnp.float32) * (1.0 / (4.0 * SOURCES))
        weighted = weight * coarse_adjoint
        dfield_h, dfield_l = halves(field_ref[source] * jnp.concatenate([weighted, weighted], axis=1))
        dline2 = dot(dfield_h, right_t)
        dline = dline2[:, :128] + dline2[:, 128:] + dot(dfield_l, right_t[:, :128])
        damp4 = dot(left_t, jnp.concatenate(halves(dline), axis=1))
        damp2 = damp4[:128] + damp4[128:]
        damp1 = damp2[:, :128] + damp2[:, 128:]
        swapped = pltpu.roll(damp1[64:], 64, 1)
        damp = damp1[:64] + jnp.where(low_w, swapped, -swapped)
        grad = pupil_ref[0] * damp - pupil_ref[1] * pltpu.roll(damp, 64, 1)
        rows = pl.ds(32 - shift_a, 64)
        grad_ref[0, rows, :] += pltpu.roll(jnp.where(low_w, grad, 0.0), 32 - shift_b, 1)
        grad_ref[1, rows, :] += pltpu.roll(jnp.where(low_w, 0.0, grad), lax.rem(96 - shift_b, 128), 1)
    grads = jnp.concatenate([grad_ref[0], grad_ref[1]], axis=0)
    folded = dot(jnp.concatenate(halves(grads), axis=1), jnp.concatenate([lanes, lanes], axis=0))
    fold_re, fold_im = folded[:FREQ], folded[FREQ:]
    packed = jnp.concatenate(
        [jnp.where(low, fold_re, -fold_im), jnp.where(low, -fold_im, -fold_re)], axis=0
    )
    packed = dot(jnp.concatenate([unfold_t, unfold_t], axis=1), jnp.concatenate(halves(packed), axis=0))
    first = my_src == 0
    edge_rows = row_ref[pl.ds(pl.multiple_of(jnp.where(first, EXT_PX - HALO, 0), HALO), HALO), :]
    mine_rows = row_ref[pl.ds(pl.multiple_of(HALO + my_src * ROWS, HALO), ROWS), :]
    tables = jnp.concatenate([edge_rows, mine_rows], axis=0)
    back = jnp.dot(tables, packed, precision=lax.Precision.HIGHEST, preferred_element_type=jnp.float32)
    goes_to = jnp.where(first, below, above)

    @pl.when(goes_to >= 0)
    def _():
        edge_ref[...] = back[:HALO].astype(jnp.bfloat16)
        send = pltpu.make_async_copy(edge_ref, sent_hbm.at[goes_to // 2], sems.at[9])
        send.start()
        send.wait()

    back_ref[...] = back[HALO:]
    keep.wait()


def make_fields(slot_pos, ints, *arrays):
    return pl.pallas_call(
        fields_kernel,
        out_shape=(
            jax.ShapeDtypeStruct((ROWS, TILE_PX), jnp.float32),
            jax.ShapeDtypeStruct((ROWS, 128), jnp.float32),
            jax.ShapeDtypeStruct((TILES // 2, HALO, 128), jnp.bfloat16),
        ),
        in_specs=[SCALARS, SCALARS] + [WHOLE] * 6 + [LEFT_THERE] * 3,
        out_specs=[LEFT_THERE, WHOLE, LEFT_THERE],
        scratch_shapes=[
            pltpu.VMEM((HALO, 128), jnp.bfloat16),
            pltpu.VMEM(GRIDS.shape, jnp.bfloat16),
            pltpu.VMEM(GRIDS.shape[::-1], jnp.bfloat16),
            pltpu.VMEM((TILE_PX, TILE_PX), jnp.bfloat16),
            pltpu.VMEM((TILE_PX, TILE_PX), jnp.float32),
            pltpu.VMEM((2, FREQ, FREQ), jnp.float32),
            pltpu.VMEM((SOURCES, GRID, 2 * GRID), jnp.float32),
            pltpu.VMEM((TILE_PX, 2 * GRID), jnp.bfloat16),
            pltpu.VMEM((2, FREQ, FREQ), jnp.float32),
            pltpu.SemaphoreType.DMA((10,)),
        ],
        compiler_params=pltpu.CompilerParams(vmem_limit_bytes=FIELDS_VMEM),
        interpret=INTERPRET,
        name="fields",
    )(slot_pos, ints, *arrays)


def steps_kernel(back_ref, col_ref, steps_hbm, edge_ref, steps_ref, sems):
    my_src = lax.axis_index("src")
    high, low = halves(-LEARN_RATE * back_ref[...])
    steps_ref[...] = dot_t(high, col_ref[...]) + dot_t(low, col_ref[...])
    keep = pltpu.make_async_copy(steps_ref, steps_hbm, sems.at[0])
    keep.start()
    at_end = my_src == SRC_DEVICES - 1
    edge_ref[...] = jnp.where(at_end, steps_ref[ROWS - HALO :, :], steps_ref[:HALO, :])
    keep.wait()


def make_steps(back, col):
    return pl.pallas_call(
        steps_kernel,
        out_shape=(
            jax.ShapeDtypeStruct((ROWS, TILE_PX), jnp.float32),
            jax.ShapeDtypeStruct((HALO, TILE_PX), jnp.float32),
        ),
        in_specs=[WHOLE, WHOLE],
        out_specs=[LEFT_THERE, WHOLE],
        scratch_shapes=[pltpu.VMEM((ROWS, TILE_PX), jnp.float32), pltpu.SemaphoreType.DMA((1,))],
        compiler_params=pltpu.CompilerParams(vmem_limit_bytes=4 * MIB),
        interpret=INTERPRET,
        name="steps",
    )(back, col)


def edge_kernel(slot_ref, got_ref, other_ref, edge_ref, col_ref, steps_in, steps_hbm, sum_ref, sems):
    my_slot, my_src, above, below = places(slot_ref)
    first = my_src == 0
    last = my_src == SRC_DEVICES - 1
    comes_from = jnp.where(first, above, below)

    @pl.when((first | last) & (comes_from >= 0))
    def _():
        place = comes_from // 2
        same_core = lax.rem(comes_from, 2) == lax.rem(my_slot, 2)
        rim = jnp.where(same_core, got_ref[place].astype(jnp.float32), other_ref[place].astype(jnp.float32))
        sum_ref[...] = edge_ref[...] - LEARN_RATE * dot_t(rim.astype(jnp.bfloat16), col_ref[...])
        start = pl.multiple_of(jnp.where(first, 0, ROWS - HALO), HALO)
        keep = pltpu.make_async_copy(sum_ref, steps_hbm.at[pl.ds(start, HALO)], sems.at[0])
        keep.start()
        keep.wait()


def add_edge(slot_pos, got, other, edge, col, steps):
    return pl.pallas_call(
        edge_kernel,
        out_shape=jax.ShapeDtypeStruct((ROWS, TILE_PX), jnp.float32),
        in_specs=[SCALARS] + [WHOLE] * 4 + [LEFT_THERE],
        out_specs=LEFT_THERE,
        scratch_shapes=[pltpu.VMEM((HALO, TILE_PX), jnp.float32), pltpu.SemaphoreType.DMA((1,))],
        input_output_aliases={5: 0},
        compiler_params=pltpu.CompilerParams(vmem_limit_bytes=4 * MIB),
        interpret=INTERPRET,
        name="edge",
    )(slot_pos, got, other, edge, col, steps)


def pupil_tables(pupil_phase):
    window = pupil_phase[32:96, 32:96]
    real = jnp.where(DISC, jnp.cos(window), 0.0) * SCALE
    imag = jnp.where(DISC, jnp.sin(window), 0.0) * SCALE
    return jnp.stack([jnp.concatenate([real, real], axis=1), jnp.concatenate([-imag, imag], axis=1)])


def own_moments(tile, col, row_table):
    half = jnp.dot(tile, col, preferred_element_type=jnp.float32)
    rows = row_table[HALO : HALO + TILE_PX]
    return lax.dot_general(
        rows, half, (((0,), (0,)), ((), ())), precision=lax.Precision.HIGHEST, preferred_element_type=jnp.float32
    )


def swap_src(value, mask):
    return lax.ppermute(value, "src", [(i, i ^ mask) for i in range(SRC_DEVICES)])


def per_device(mask_tiles, slot_pos, src_shift, src_weight, pupil_phase, target):
    ints = pack_sources(src_shift, src_weight)
    ints = ints + swap_src(ints, 4)
    col = jnp.asarray(COL)
    row_table = lax.optimization_barrier(jnp.asarray(ROW_F32))
    tile = mask_tiles[0]
    got = lax.all_to_all(make_rims(slot_pos, tile, col), "tile", 0, 0, tiled=True)
    ints, col_after, small, grids = lax.optimization_barrier((ints, col, jnp.asarray(SMALL), jnp.asarray(GRIDS)))
    ints = ints + swap_src(ints, 1) + swap_src(ints, 2) + swap_src(ints, 3)
    own = own_moments(tile, col_after, row_table)
    flipped, right_t = flip_tables(small, grids)
    resist, back, sent = make_fields(
        slot_pos, ints, got, own, pupil_tables(pupil_phase), small, right_t, row_table, grids, flipped, target[0]
    )
    cores = [[2 * chip + core for chip in range(TILES // 2)] for core in range(2)]
    got = lax.all_to_all(sent, "tile", 0, 0, tiled=True, axis_index_groups=cores)
    steps, edge = make_steps(back, col)
    got, edge = lax.optimization_barrier((got, edge))
    other = lax.ppermute(got, "tile", [(i, i ^ 1) for i in range(TILES)])
    return (resist[None], add_edge(slot_pos, got, other, edge, col, steps)[None])


def solution(mesh):
    return jax.shard_map(
        per_device,
        mesh=mesh,
        in_specs=(P("tile", None, None), P(), P("src", None), P("src"), P(), P("tile", None, None)),
        out_specs=(P("tile", "src", None), P("tile", "src", None)),
        check_vma=False,
    )
```
